32 devices in a mesh: rep: 8 (over z, x), tp: 4 (over y, core).
Axes of the slice: x: 2, y: 2, z: 4, core: 2. Of those that a mesh axis runs over, the one named last changes fastest.
Arguments:
- weight: bfloat16 [8, 2048, 7168], P('rep', None, 'tp'), may hold values from -6 to 6
- tokens: bfloat16 [8, 2, 512, 2048], P('rep'), may hold values from -6 to 6
- cotangent: bfloat16 [8, 2, 512, 7168], P('rep', None, None, 'tp'), may hold values from -6 to 6
- batch_order: int32 [8, 2], P('rep'), may hold values from 0 to 1, each once within a row
- step_index: int32 [1], replicated, may hold values from 0 to 999
Outputs:
- averaged: bfloat16 [8, 2048, 7168], P('rep', None, 'tp')
- losses: float32 [8, 2], P('rep')
The draws below stay inside these ranges and needn't reach their ends.
Inputs may be any that keep to these rules, and one draw needn't show every extreme that they name: `batch_order`: each row lists 0 to 1 once.
All inputs are finite; a program needn't handle non-finite values.
Results may differ from the reference program's by a relative error of at most 0.009.
Values may be sent and summed in bfloat16 or wider, within the bound.
No kernel may reach another device: no remote copies, remote signals or barrier semaphores. Data moves between devices by JAX's collectives and lax.ppermute only.
A program may use at most 256 MiB of HBM per device.

```python
import jax
import jax.numpy as jnp
from jax import lax

D = 2048
FF = 7168
TOK = 512
STEPS = 2
REPLICAS = 8
N_REP = 8


def steps_of(key, extent, shards, least, largest):
    def one(axis_at, blocks):
        draws = jax.random.uniform(jax.random.fold_in(jax.random.fold_in(key, 6), axis_at), (blocks,), jnp.float32, least / len(shards), largest / len(shards))
        return jnp.repeat(jnp.exp(draws), extent[axis_at] // blocks).reshape((-1,) + (1,) * (len(extent) - axis_at - 1))

    factor_of = one(*shards[0])
    for cut in shards[1:]:
        factor_of = factor_of * one(*cut)
    return factor_of


def gaussian(key, shape, scale, limit, pieces=(), dtype=jnp.bfloat16):
    result = jax.random.normal(key, shape, jnp.float32) * scale
    if len(pieces) > 0:
        result = steps_of(key, shape, pieces, -0.22, 0.18) * result
    return jnp.clip(result, min=-limit, max=limit).astype(dtype)


def setup_inputs(seed: int = 0) -> dict:
    seeds = jax.random.split(jax.random.key(seed), 6)
    return {
        "weight": gaussian(seeds[0], (REPLICAS, D, FF), 1.0, 6.0, ((0, 8), (2, 4))),
        "tokens": gaussian(seeds[1], (REPLICAS, STEPS, TOK, D), 1.0, 6.0, ((0, 8),)),
        "cotangent": gaussian(seeds[2], (REPLICAS, STEPS, TOK, FF), 1.0, 6.0, ((0, 8), (3, 4))),
        "batch_order": jax.vmap(lambda own: jax.random.permutation(own, STEPS))(jax.random.split(seeds[3], REPLICAS)).reshape((REPLICAS, STEPS)).astype(jnp.int32),
        "step_index": jax.random.randint(seeds[4], (1,), 0, 1000).astype(jnp.int32),
    }


beta_first = 0.9
beta_second = 0.95
learn_rate = 0.05
decay_rate = 0.1
adam_eps = 1e-05
norm_eps = 1e-06

def local_chain(operands):
    weight, tokens, cotangent, order = operands
    width_scale = D ** (-0.5)
    master = weight.astype(jnp.float32)
    moment = jnp.zeros(master.shape, jnp.float32)
    second = jnp.zeros(master.shape, jnp.float32)
    losses = []
    for local_step in range(STEPS):
        chosen = order[local_step].astype(jnp.int32)
        inputs = lax.dynamic_index_in_dim(tokens, chosen, 0, keepdims=False)
        target = lax.dynamic_index_in_dim(cotangent, chosen, 0, keepdims=False).astype(jnp.float32)
        current = master.astype(jnp.bfloat16)
        hidden = jnp.dot(inputs, current, preferred_element_type=jnp.float32) * width_scale
        squares = lax.optimization_barrier(jnp.sum(hidden * hidden, axis=1))
        inner = lax.optimization_barrier(jnp.sum(target * hidden, axis=1))
        radius = jnp.sqrt(squares / FF + norm_eps)
        losses.append(jnp.mean(inner / radius))
        grad_rows = (target / radius[:, None] - hidden * (inner / (FF * radius ** 3))[:, None]) / TOK
        grad_rows = grad_rows.astype(jnp.bfloat16)
        gradient = jnp.dot(inputs.T, grad_rows, preferred_element_type=jnp.float32) * width_scale
        moment = beta_first * moment + (1.0 - beta_first) * gradient
        second = beta_second * second + (1.0 - beta_second) * gradient * gradient
        moment_hat = moment / (1.0 - beta_first ** (local_step + 1))
        second_hat = second / (1.0 - beta_second ** (local_step + 1))
        master = master - learn_rate * (moment_hat / (jnp.sqrt(second_hat) + adam_eps) + decay_rate * master)
    return (master.astype(jnp.bfloat16), jnp.stack(losses))

def reference(weight, tokens, cotangent, batch_order, step_index):
    final_weight, losses = lax.map(local_chain, (weight, tokens, cotangent, batch_order))
    levels = N_REP.bit_length() - 1
    distance = (2 ** (step_index[0] % levels)).astype(jnp.int32)
    peer_weight = jnp.roll(final_weight, distance, axis=0)
    averaged = ((final_weight.astype(jnp.float32) + peer_weight.astype(jnp.float32)) * 0.5).astype(jnp.bfloat16)
    return (averaged, losses)
```

```python
import functools

import jax
import jax.numpy as jnp
from jax import lax
from jax.experimental import pallas as pl
from jax.experimental.pallas import tpu as pltpu
from jax.sharding import PartitionSpec as P

beta_first = 0.9
beta_second = 0.95
learn_rate = 0.05
decay_rate = 0.1
adam_eps = 1e-05
norm_eps = 1e-06

F32 = jnp.float32
BF16 = jnp.bfloat16
VMEM_LIMIT = 60 * 1024 * 1024


def width_block(columns):
    for block in (256, 128):
        if columns % block == 0:
            return block
    return columns


def lane_fold(values):
    total = values[:, :128]
    for at in range(128, values.shape[1], 128):
        total = total + values[:, at : at + 128]
    return total


def add_stats(step, squares, inner, hidden, target):
    part_squares = lane_fold(hidden * hidden)
    part_inner = lane_fold(target * hidden)

    @pl.when(step == 0)
    def _():
        squares[...] = part_squares
        inner[...] = part_inner

    @pl.when(step > 0)
    def _():
        squares[...] += part_squares
        inner[...] += part_inner


def write_stats(stats_ref, squares, inner):
    stats_ref[0:1, :] = jnp.sum(squares[...].T, axis=0, keepdims=True)
    stats_ref[1:2, :] = jnp.sum(inner[...].T, axis=0, keepdims=True)


def token_factors(stats, units, tokens):
    squares, inner = stats[0:1, :], stats[1:2, :]
    radius = jnp.sqrt(squares / units + norm_eps)
    loss = jnp.sum(inner / radius, axis=1, keepdims=True) / tokens
    by_target = 1.0 / (radius * tokens)
    by_hidden = inner / (units * radius * radius * radius * tokens)
    pad = jnp.zeros((6, stats.shape[1]), F32)
    columns = jnp.concatenate([by_target, by_hidden, pad], axis=0).T
    return columns, loss


def forward_kernel(order, x_ref, w_ref, c_ref, h_ref, xt_ref, stats_ref, squares, inner, *, scale):
    step = pl.program_id(0)
    hidden = jnp.dot(x_ref[...], w_ref[...], preferred_element_type=F32) * scale
    h_ref[...] = hidden
    add_stats(step, squares, inner, hidden, c_ref[...].astype(F32))

    @pl.when(step == 0)
    def _():
        xt_ref[...] = x_ref[...].T

    @pl.when(step == pl.num_programs(0) - 1)
    def _():
        write_stats(stats_ref, squares, inner)


def forward(order, tokens, weight, target, units):
    steps, count, width = tokens.shape
    columns = weight.shape[1]
    block = width_block(columns)
    return pl.pallas_call(
        functools.partial(forward_kernel, scale=width**-0.5),
        out_shape=(
            jax.ShapeDtypeStruct((count, columns), F32),
            jax.ShapeDtypeStruct((width, count), BF16),
            jax.ShapeDtypeStruct((2, count), F32),
        ),
        grid_spec=pltpu.PrefetchScalarGridSpec(
            num_scalar_prefetch=1,
            grid=(columns // block,),
            in_specs=[
                pl.BlockSpec((None, count, width), lambda j, o: (o[0], 0, 0)),
                pl.BlockSpec((width, block), lambda j, o: (0, j)),
                pl.BlockSpec((None, count, block), lambda j, o: (o[0], 0, j)),
            ],
            out_specs=(
                pl.BlockSpec((count, block), lambda j, o: (0, j)),
                pl.BlockSpec((width, count), lambda j, o: (0, 0)),
                pl.BlockSpec((2, count), lambda j, o: (0, 0)),
            ),
            scratch_shapes=[pltpu.VMEM((count, 128), F32), pltpu.VMEM((count, 128), F32)],
        ),
        compiler_params=pltpu.CompilerParams(vmem_limit_bytes=VMEM_LIMIT),
        name="forward_first",
    )(order, tokens, weight, target)


def middle_kernel(
    order, stats_in, xt_ref, x_ref, w_ref, h_ref, c1_ref, c2_ref,
    g_ref, h2_ref, xt2_ref, stats_ref, loss_ref, factors, squares, inner, *, scale, units, rows,
):
    step = pl.program_id(0)
    count = h_ref.shape[0]

    @pl.when(step == 0)
    def _():
        columns, loss = token_factors(stats_in[...], units, count)
        factors[...] = columns
        loss_ref[...] = jnp.broadcast_to(loss, loss_ref.shape)
        xt2_ref[...] = x_ref[...].T

    by_target = factors[:, 0:1]
    by_hidden = factors[:, 1:2]
    grad_rows = (c1_ref[...].astype(F32) * by_target - h_ref[...] * by_hidden).astype(BF16)
    total = None
    for at in range(0, w_ref.shape[0], rows):
        part = pl.ds(at, rows)
        gradient = jnp.dot(xt_ref[part, :], grad_rows, preferred_element_type=F32) * scale
        g_ref[part, :] = gradient.astype(BF16)
        master = w_ref[part, :].astype(F32)
        moved = gradient / (jnp.abs(gradient) + adam_eps)
        current = (master - learn_rate * (moved + decay_rate * master)).astype(BF16)
        term = jnp.dot(x_ref[:, part], current, preferred_element_type=F32)
        total = term if total is None else total + term
    hidden = total * scale
    h2_ref[...] = hidden
    add_stats(step, squares, inner, hidden, c2_ref[...].astype(F32))

    @pl.when(step == pl.num_programs(0) - 1)
    def _():
        write_stats(stats_ref, squares, inner)


def middle(order, stats, flipped, tokens, weight, hidden, target, units):
    steps, count, width = tokens.shape
    columns = weight.shape[1]
    block = width_block(columns)
    return pl.pallas_call(
        functools.partial(middle_kernel, scale=width**-0.5, units=units, rows=min(512, width)),
        out_shape=(
            jax.ShapeDtypeStruct((width, columns), BF16),
            jax.ShapeDtypeStruct((count, columns), F32),
            jax.ShapeDtypeStruct((width, count), BF16),
            jax.ShapeDtypeStruct((2, count), F32),
            jax.ShapeDtypeStruct((1, 128), F32),
        ),
        grid_spec=pltpu.PrefetchScalarGridSpec(
            num_scalar_prefetch=1,
            grid=(columns // block,),
            in_specs=[
                pl.BlockSpec((2, count), lambda j, o: (0, 0)),
                pl.BlockSpec((width, count), lambda j, o: (0, 0)),
                pl.BlockSpec((None, count, width), lambda j, o: (o[1], 0, 0)),
                pl.BlockSpec((width, block), lambda j, o: (0, j)),
                pl.BlockSpec((count, block), lambda j, o: (0, j)),
                pl.BlockSpec((None, count, block), lambda j, o: (o[0], 0, j)),
                pl.BlockSpec((None, count, block), lambda j, o: (o[1], 0, j)),
            ],
            out_specs=(
                pl.BlockSpec((width, block), lambda j, o: (0, j)),
                pl.BlockSpec((count, block), lambda j, o: (0, j)),
                pl.BlockSpec((width, count), lambda j, o: (0, 0)),
                pl.BlockSpec((2, count), lambda j, o: (0, 0)),
                pl.BlockSpec((1, 128), lambda j, o: (0, 0)),
            ),
            scratch_shapes=[
                pltpu.VMEM((count, 8), F32),
                pltpu.VMEM((count, 128), F32),
                pltpu.VMEM((count, 128), F32),
            ],
        ),
        compiler_params=pltpu.CompilerParams(vmem_limit_bytes=VMEM_LIMIT),
        name="middle",
    )(order, stats, flipped, tokens, weight, hidden, target, target)


def last_kernel(
    order, stats_in, xt_ref, w_ref, g_ref, h_ref, c_ref, final_ref, loss_ref, grad_rows, *, scale, units
):
    count = h_ref.shape[0]

    @pl.when(pl.program_id(0) == 0)
    def _():
        columns, loss = token_factors(stats_in[...], units, count)
        loss_ref[...] = jnp.broadcast_to(loss, loss_ref.shape)
        grad_rows[...] = (
            c_ref[...].astype(F32) * columns[:, 0:1] - h_ref[...] * columns[:, 1:2]
        ).astype(BF16)

    gradient = jnp.dot(xt_ref[...], grad_rows[...], preferred_element_type=F32) * scale
    first = g_ref[...].astype(F32)
    master = w_ref[...].astype(F32)
    master = master - learn_rate * (first / (jnp.abs(first) + adam_eps) + decay_rate * master)
    moment = beta_first * ((1.0 - beta_first) * first) + (1.0 - beta_first) * gradient
    second = beta_second * ((1.0 - beta_second) * first * first) + (1.0 - beta_second) * gradient * gradient
    moment_hat = moment / (1.0 - beta_first**2)
    second_hat = second / (1.0 - beta_second**2)
    master = master - learn_rate * (
        moment_hat / (jnp.sqrt(second_hat) + adam_eps) + decay_rate * master
    )
    final_ref[...] = master.astype(BF16)


def last(order, stats, flipped, weight, gradient, hidden, target, units, chunk, block):
    width, count = flipped.shape
    rows = min(256, width)
    return pl.pallas_call(
        functools.partial(last_kernel, scale=width**-0.5, units=units),
        out_shape=(
            jax.ShapeDtypeStruct((width, block), BF16),
            jax.ShapeDtypeStruct((1, 128), F32),
        ),
        grid_spec=pltpu.PrefetchScalarGridSpec(
            num_scalar_prefetch=1,
            grid=(width // rows,),
            in_specs=[
                pl.BlockSpec((2, count), lambda i, o: (0, 0)),
                pl.BlockSpec((rows, count), lambda i, o: (i, 0)),
                pl.BlockSpec((rows, block), lambda i, o: (i, chunk)),
                pl.BlockSpec((rows, block), lambda i, o: (i, chunk)),
                pl.BlockSpec((count, block), lambda i, o: (0, chunk)),
                pl.BlockSpec((None, count, block), lambda i, o: (o[1], 0, chunk)),
            ],
            out_specs=(
                pl.BlockSpec((rows, block), lambda i, o: (i, 0)),
                pl.BlockSpec((1, 128), lambda i, o: (0, 0)),
            ),
            scratch_shapes=[pltpu.VMEM((count, block), BF16)],
        ),
        compiler_params=pltpu.CompilerParams(vmem_limit_bytes=VMEM_LIMIT // 4),
        cost_estimate=pl.CostEstimate(
            flops=2 * width * count * block,
            bytes_accessed=2 * width * (3 * block + count) + 6 * count * block,
            transcendentals=3 * width * block,
        ),
        name="last",
    )(order, stats, flipped, weight, gradient, hidden, target)


def mean_kernel(own_ref, peer_ref, *refs):
    out_ref = refs[-1]
    out_ref[...] = ((own_ref[...].astype(F32) + peer_ref[...].astype(F32)) * 0.5).astype(BF16)


def mean_into(out, own, peer, columns, chunk):
    width, block = own.shape
    rows = min(512, width)
    spec = pl.BlockSpec((rows, block), lambda i: (i, 0))
    return pl.pallas_call(
        mean_kernel,
        out_shape=jax.ShapeDtypeStruct((width, columns), BF16),
        grid=(width // rows,),
        in_specs=[spec, spec] + ([] if out is None else [pl.BlockSpec(memory_space=pl.ANY)]),
        out_specs=pl.BlockSpec((rows, block), lambda i: (i, chunk)),
        input_output_aliases={} if out is None else {2: 0},
        compiler_params=pltpu.CompilerParams(vmem_limit_bytes=VMEM_LIMIT // 4),
        cost_estimate=pl.CostEstimate(
            flops=2 * width * block, bytes_accessed=6 * width * block, transcendentals=0
        ),
        name="mean",
    )(*([own, peer] + ([] if out is None else [out])))


def shifted(array, axis, by):
    devices = lax.axis_size(axis)
    return lax.ppermute(array, axis, [(i, (i + by) % devices) for i in range(devices)])


def shards(weight, tokens, cotangent, batch_order, step_index):
    weight, tokens, target, order = weight[0], tokens[0], cotangent[0], batch_order[0]
    width, columns = weight.shape
    units = columns * lax.axis_size("tp")
    levels = lax.axis_size("rep").bit_length() - 1
    hop_level = step_index[0] % levels
    block = width_block(columns)

    hidden, flipped, stats = forward(order, tokens, weight, target, units)
    stats = lax.psum(stats, "tp")
    gradient, hidden, flipped, stats, loss_first = middle(
        order, stats, flipped, tokens, weight, hidden, target, units
    )
    stats = lax.psum(stats, "tp")

    def gossip(exponent):
        def run(order, stats, flipped, weight, gradient, hidden, target):
            finals, peers = [], []
            for chunk in range(columns // block):
                final, loss = last(
                    order, stats, flipped, weight, gradient, hidden, target, units, chunk, block
                )
                finals.append(final)
                peers.append(shifted(final, "rep", 2**exponent))
                if chunk == 0:
                    loss_second = loss
            out = None
            for chunk, (final, peer) in enumerate(zip(finals, peers)):
                out = mean_into(out, final, peer, columns, chunk)
            return out, loss_second

        return run

    averaged, loss_second = lax.switch(
        hop_level,
        [gossip(exponent) for exponent in range(levels)],
        order, stats, flipped, weight, gradient, hidden, target,
    )
    losses = jnp.concatenate([loss_first[:, :1], loss_second[:, :1]], axis=1)
    return (averaged[None], losses)


def solution(mesh):
    placed = (
        P("rep", None, "tp"),
        P("rep", None, None, None),
        P("rep", None, None, "tp"),
        P("rep", None),
        P(),
    )
    return jax.shard_map(
        shards,
        mesh=mesh,
        in_specs=placed,
        out_specs=(P("rep", None, "tp"), P("rep", None)),
        check_vma=False,
    )
```

```python
import functools

import jax
import jax.numpy as jnp
from jax import lax
from jax.experimental import pallas as pl
from jax.experimental.pallas import tpu as pltpu
from jax.sharding import PartitionSpec as P


beta_first = 0.9
beta_second = 0.95
learn_rate = 0.05
decay_rate = 0.1
adam_eps = 1e-05
norm_eps = 1e-06

F32 = jnp.float32
BF16 = jnp.bfloat16
KERNEL_VMEM = 16 * 1024 * 1024
ROWS = 512


def width_block(columns):
    for block in (256, 128):
        if columns % block == 0:
            return block
    return columns


def chunks_of(columns):
    block = width_block(columns)
    sizes = [block] * (columns // block)
    if block == 256 and len(sizes) > 1:
        sizes = [128] + sizes[1:] + [128]
    pieces = []
    low = 0
    for size in sizes:
        pieces.append((low, size))
        low += size
    return pieces


def lane_fold(values):
    total = values[:, :128]
    for at in range(128, values.shape[1], 128):
        total = total + values[:, at : at + 128]
    return total


def write_stats(stats_ref, squares, inner):
    stats_ref[0:1, :] = jnp.sum(squares[...].T, axis=0, keepdims=True)
    stats_ref[1:2, :] = jnp.sum(inner[...].T, axis=0, keepdims=True)


def token_factors(stats, units, tokens):
    squares, inner = stats[0:1, :], stats[1:2, :]
    radius = jnp.sqrt(squares / units + norm_eps)
    loss = jnp.sum(inner / radius, axis=1, keepdims=True) / tokens
    by_target = 1.0 / (radius * tokens)
    by_hidden = inner / (units * radius * radius * radius * tokens)
    pad = jnp.zeros((6, stats.shape[1]), F32)
    columns = jnp.concatenate([by_target, by_hidden, pad], axis=0).T
    return columns, loss


def forward_kernel(
    order, x_hbm, w_hbm, c_hbm,
    h_ref, xt_ref, stats_ref, x_ref, w_ref, c_ref, squares, inner, x_sem, w_sem, c_sem, *, scale, block,
):
    width, columns = w_ref.shape
    blocks = columns // block
    first, second = order[0], order[1]
    x_copies = [
        pltpu.make_async_copy(x_hbm.at[chosen], x_ref.at[at], x_sem.at[at])
        for at, chosen in enumerate((first, second))
    ]
    c_copies = [
        pltpu.make_async_copy(c_hbm.at[chosen], c_ref.at[at], c_sem.at[at])
        for at, chosen in enumerate((first, second))
    ]

    def w_copy(at):
        part = pl.ds(pl.multiple_of(at * block, block), block)
        return pltpu.make_async_copy(w_hbm.at[:, part], w_ref.at[:, part], w_sem.at[at])

    x_copies[0].start()
    w_copy(0).start()
    c_copies[0].start()
    for at in range(1, blocks):
        w_copy(at).start()
    x_copies[1].start()
    c_copies[1].start()
    squares[...] = jnp.zeros_like(squares)
    inner[...] = jnp.zeros_like(inner)
    piece = width // blocks // 128 * 128
    x_copies[0].wait()
    c_copies[0].wait()

    def one(at, carry):
        w_copy(at).wait()
        part = pl.ds(pl.multiple_of(at * block, block), block)
        hidden = jnp.dot(x_ref[0], w_ref[:, part], preferred_element_type=F32) * scale
        h_ref[:, part] = hidden
        target = c_ref[0, :, part].astype(F32)
        squares[...] += lane_fold(hidden * hidden)
        inner[...] += lane_fold(target * hidden)
        flip = pl.ds(pl.multiple_of(at * piece, 128), piece)
        xt_ref[flip, :] = x_ref[0, :, flip].T
        return carry

    lax.fori_loop(0, blocks, one, 0)
    if piece * blocks < width:
        xt_ref[piece * blocks :, :] = x_ref[0, :, piece * blocks :].T
    write_stats(stats_ref, squares, inner)
    x_copies[1].wait()
    c_copies[1].wait()


def forward(order, tokens, weight, target):
    steps, count, width = tokens.shape
    columns = weight.shape[1]
    block = width_block(columns)
    blocks = columns // block
    whole = pl.BlockSpec(memory_space=pltpu.VMEM)
    return pl.pallas_call(
        functools.partial(forward_kernel, scale=width**-0.5, block=block),
        out_shape=(
            pltpu.VMEM((count, columns), F32),
            pltpu.VMEM((width, count), BF16),
            jax.ShapeDtypeStruct((2, count), F32),
            pltpu.VMEM(tokens.shape, BF16),
            pltpu.VMEM(weight.shape, BF16),
            pltpu.VMEM(target.shape, BF16),
        ),
        in_specs=[pl.BlockSpec(memory_space=pltpu.SMEM)] + [pl.BlockSpec(memory_space=pl.ANY)] * 3,
        out_specs=(whole,) * 6,
        scratch_shapes=[
            pltpu.VMEM((count, 128), F32),
            pltpu.VMEM((count, 128), F32),
            pltpu.SemaphoreType.DMA((steps,)),
            pltpu.SemaphoreType.DMA((blocks,)),
            pltpu.SemaphoreType.DMA((steps,)),
        ],
        compiler_params=pltpu.CompilerParams(vmem_limit_bytes=KERNEL_VMEM),
        name="forward_first",
    )(order, tokens, weight, target)


def middle_kernel(
    parts, xt_ref, x_ref, w_ref, h_ref, c_ref,
    g_ref, h2_ref, xt2_ref, stats_ref, loss_ref, factors, squares, inner, *, scale, units, rows, block,
):
    count, columns = h_ref.shape
    width = w_ref.shape[0]
    blocks = columns // block
    factors[...], loss = token_factors(tree_sum([part[...] for part in parts]), units, count)
    loss_ref[...] = jnp.broadcast_to(loss, loss_ref.shape)
    squares[...] = jnp.zeros_like(squares)
    inner[...] = jnp.zeros_like(inner)
    piece = width // blocks // 128 * 128

    def one(at, carry):
        cols = pl.ds(pl.multiple_of(at * block, block), block)
        grad_rows = (
            c_ref[0, :, cols].astype(F32) * factors[:, 0:1] - h_ref[:, cols] * factors[:, 1:2]
        ).astype(BF16)
        total = None
        for low in range(0, width, rows):
            part = pl.ds(low, rows)
            gradient = jnp.dot(xt_ref[part, :], grad_rows, preferred_element_type=F32) * scale
            g_ref[part, cols] = gradient.astype(BF16)
            master = w_ref[part, cols].astype(F32)
            moved = gradient / (jnp.abs(gradient) + adam_eps)
            current = (master - learn_rate * (moved + decay_rate * master)).astype(BF16)
            term = jnp.dot(x_ref[1, :, part], current, preferred_element_type=F32)
            total = term if total is None else total + term
        hidden = total * scale
        h2_ref[:, cols] = hidden
        squares[...] += lane_fold(hidden * hidden)
        inner[...] += lane_fold(c_ref[1, :, cols].astype(F32) * hidden)
        flip = pl.ds(pl.multiple_of(at * piece, 128), piece)
        xt2_ref[flip, :] = x_ref[1, :, flip].T
        return carry

    lax.fori_loop(0, blocks, one, 0)
    if piece * blocks < width:
        xt2_ref[piece * blocks :, :] = x_ref[1, :, piece * blocks :].T
    write_stats(stats_ref, squares, inner)


def middle(stats, flipped, tokens, weight, hidden, target, units):
    _, count, width = tokens.shape
    columns = weight.shape[1]
    block = width_block(columns)
    whole = pl.BlockSpec(memory_space=pltpu.VMEM)
    return pl.pallas_call(
        functools.partial(
            middle_kernel, scale=width**-0.5, units=units, rows=min(ROWS, width), block=block
        ),
        out_shape=(
            pltpu.VMEM((width, columns), BF16),
            pltpu.VMEM((count, columns), F32),
            pltpu.VMEM((width, count), BF16),
            jax.ShapeDtypeStruct((2, count), F32),
            jax.ShapeDtypeStruct((1, 128), F32),
        ),
        in_specs=[[whole] * len(stats)] + [whole] * 5,
        out_specs=(whole,) * 5,
        scratch_shapes=[
            pltpu.VMEM((count, 8), F32),
            pltpu.VMEM((count, 128), F32),
            pltpu.VMEM((count, 128), F32),
        ],
        compiler_params=pltpu.CompilerParams(vmem_limit_bytes=KERNEL_VMEM),
        name="middle",
    )(stats, flipped, tokens, weight, hidden, target)


def last_kernel(
    parts, xt_ref, w_ref, g_ref, h_ref, c_ref, final_ref, loss_ref,
    *, scale, units, low, block, rows,
):
    count = h_ref.shape[0]
    cols = slice(low, low + block)
    columns, loss = token_factors(tree_sum([part[...] for part in parts]), units, count)
    loss_ref[...] = jnp.broadcast_to(loss, loss_ref.shape)
    grad_rows = (
        c_ref[1, :, cols].astype(F32) * columns[:, 0:1] - h_ref[:, cols] * columns[:, 1:2]
    ).astype(BF16)
    first_moment = beta_first * (1.0 - beta_first) / (1.0 - beta_first**2)
    fresh_moment = (1.0 - beta_first) / (1.0 - beta_first**2)
    first_second = beta_second * (1.0 - beta_second) / (1.0 - beta_second**2)
    fresh_second = (1.0 - beta_second) / (1.0 - beta_second**2)
    keep = 1.0 - learn_rate * decay_rate

    def one(at, carry):
        part = pl.ds(pl.multiple_of(at * rows, rows), rows)
        gradient = jnp.dot(xt_ref[part, :], grad_rows, preferred_element_type=F32) * scale
        first = g_ref[part, cols].astype(F32)
        master = w_ref[part, cols].astype(F32)
        master = keep * master - learn_rate * (first / (jnp.abs(first) + adam_eps))
        moment = first_moment * first + fresh_moment * gradient
        second = first_second * (first * first) + fresh_second * (gradient * gradient)
        master = keep * master - learn_rate * (moment / (jnp.sqrt(second) + adam_eps))
        final_ref[part, :] = master.astype(BF16)
        return carry

    lax.fori_loop(0, xt_ref.shape[0] // rows, one, 0)


def last(stats, flipped, weight, gradient, hidden, target, units, low, block):
    width, count = flipped.shape
    whole = pl.BlockSpec(memory_space=pltpu.VMEM)
    return pl.pallas_call(
        functools.partial(
            last_kernel, scale=width**-0.5, units=units, low=low, block=block, rows=min(256, width)
        ),
        out_shape=(
            pltpu.VMEM((width, block), BF16),
            jax.ShapeDtypeStruct((1, 128), F32),
        ),
        in_specs=[[whole] * len(stats)] + [whole] * 5,
        out_specs=(whole,) * 2,
        compiler_params=pltpu.CompilerParams(vmem_limit_bytes=KERNEL_VMEM),
        cost_estimate=pl.CostEstimate(
            flops=2 * width * count * block,
            bytes_accessed=2 * width * (3 * block + count) + 6 * count * block,
            transcendentals=3 * width * block,
        ),
        name="last",
    )(stats, flipped, weight, gradient, hidden, target)


def mean_kernel(own_ref, peer_ref, *refs, low, rows):
    out_ref, buffer, sems = refs[-3:]
    width, block = own_ref.shape
    copies = []
    for at in range(width // rows):
        part = slice(at * rows, (at + 1) * rows)
        buffer[part, :] = (
            (own_ref[part, :].astype(F32) + peer_ref[part, :].astype(F32)) * 0.5
        ).astype(BF16)
        copy = pltpu.make_async_copy(
            buffer.at[part, :], out_ref.at[part, low : low + block], sems.at[at]
        )
        copy.start()
        copies.append(copy)
    for copy in copies:
        copy.wait()


def mean_into(out, own, peer, columns, low):
    width, block = own.shape
    rows = min(512, width)
    whole = pl.BlockSpec(memory_space=pltpu.VMEM)
    anywhere = pl.BlockSpec(memory_space=pl.ANY)
    return pl.pallas_call(
        functools.partial(mean_kernel, low=low, rows=rows),
        out_shape=jax.ShapeDtypeStruct((width, columns), BF16),
        in_specs=[whole, whole] + ([] if out is None else [anywhere]),
        out_specs=anywhere,
        scratch_shapes=[
            pltpu.VMEM((width, block), BF16),
            pltpu.SemaphoreType.DMA((width // rows,)),
        ],
        input_output_aliases={} if out is None else {2: 0},
        compiler_params=pltpu.CompilerParams(vmem_limit_bytes=KERNEL_VMEM),
        cost_estimate=pl.CostEstimate(
            flops=2 * width * block, bytes_accessed=6 * width * block, transcendentals=0
        ),
        name="mean",
    )(*([own, peer] + ([] if out is None else [out])))


def tree_sum(parts):
    while len(parts) > 1:
        parts = [parts[at] + parts[at + 1] for at in range(0, len(parts), 2)]
    return parts[0]


def everyones(array, axis):
    devices = lax.axis_size(axis)
    if devices & (devices - 1):
        return [lax.psum(array, axis)]
    return [array] + [
        lax.ppermute(array, axis, [(i, i ^ flip) for i in range(devices)])
        for flip in range(1, devices)
    ]


def shifted(array, axis, by):
    devices = lax.axis_size(axis)
    return lax.ppermute(array, axis, [(i, (i + by) % devices) for i in range(devices)])


def shards(weight, tokens, cotangent, batch_order, step_index):
    weight, tokens, target, order = weight[0], tokens[0], cotangent[0], batch_order[0]
    _, columns = weight.shape
    units = columns * lax.axis_size("tp")
    levels = lax.axis_size("rep").bit_length() - 1
    hop_level = step_index[0] % levels

    pieces = chunks_of(columns)

    def chain(exponent):
        def run(order, tokens, weight, target):
            hidden, flipped, stats, tokens, weight, target = forward(order, tokens, weight, target)
            stats = everyones(stats, "tp")
            gradient, hidden, flipped, stats, loss_first = middle(
                stats, flipped, tokens, weight, hidden, target, units
            )
            stats = everyones(stats, "tp")
            finals, peers = [], []
            for at, (low, size) in enumerate(pieces):
                final, loss = last(
                    stats, flipped, weight, gradient, hidden, target, units, low, size
                )
                loss_second = loss if at == 0 else loss_second
                finals.append(final)
                peers.append(shifted(final, "rep", 2**exponent))
            out = None
            for (low, _), final, peer in zip(pieces, finals, peers):
                out = mean_into(out, final, peer, columns, low)
            return out, jnp.concatenate([loss_first[:, :1], loss_second[:, :1]], axis=1)

        return run

    averaged, losses = lax.switch(
        hop_level, [chain(exponent) for exponent in range(levels)], order, tokens, weight, target
    )
    return (averaged[None], losses)


def solution(mesh):
    placed = (
        P("rep", None, "tp"),
        P("rep", None, None, None),
        P("rep", None, None, "tp"),
        P("rep", None),
        P(),
    )
    return jax.shard_map(
        shards,
        mesh=mesh,
        in_specs=placed,
        out_specs=(P("rep", None, "tp"), P("rep", None)),
        check_vma=False,
    )
```

```python
import functools

import jax
import jax.numpy as jnp
from jax import lax
from jax.experimental import pallas as pl
from jax.experimental.pallas import tpu as pltpu
from jax.sharding import PartitionSpec as P


beta_first = 0.9
beta_second = 0.95
learn_rate = 0.05
decay_rate = 0.1
adam_eps = 1e-05
norm_eps = 1e-06
tiny_square = 1e-30

F32 = jnp.float32
BF16 = jnp.bfloat16
KERNEL_VMEM = 16 * 1024 * 1024
ROWS = 256
LANES = 128
TOKEN_ROWS = 64
PIECE_CELLS = 256 * 256
MEAN_CELLS = 128 * 256
PIECE_COLUMNS = 512
AHEAD = 3


def width_block(columns):
    for block in (256, 128):
        if columns % block == 0:
            return block
    return columns


def chunks_of(columns):
    if columns % LANES or columns <= 2 * LANES:
        return [(0, columns)]
    sizes = [LANES]
    left = columns - 2 * LANES
    while left > 0:
        sizes.append(min(PIECE_COLUMNS, left))
        left -= sizes[-1]
    sizes.append(LANES)
    pieces = []
    low = 0
    for size in sizes:
        pieces.append((low, size))
        low += size
    return pieces


def lane_fold(values):
    total = values[:, :128]
    for at in range(128, values.shape[1], 128):
        total = total + values[:, at : at + 128]
    return total


def write_stats(stats_ref, squares, inner):
    stats_ref[0:1, :] = jnp.sum(squares[...].T, axis=0, keepdims=True)
    stats_ref[1:2, :] = jnp.sum(inner[...].T, axis=0, keepdims=True)


def token_factors(stats, units, tokens):
    squares, inner = stats[0:1, :], stats[1:2, :]
    radius = jnp.sqrt(squares / units + norm_eps)
    loss = jnp.sum(inner / radius, axis=1, keepdims=True) / tokens
    by_target = 1.0 / (radius * tokens)
    by_hidden = inner / (units * radius * radius * radius * tokens)
    pad = jnp.zeros((6, stats.shape[1]), F32)
    columns = jnp.concatenate([by_target, by_hidden, pad], axis=0).T
    return columns, loss


def spread(column, lanes):
    return jnp.broadcast_to(column, (column.shape[0], lanes))


def forward_kernel(
    order, x_hbm, w_hbm, c_hbm,
    h_ref, xt_ref, stats_ref, x_ref, w_ref, c_ref, squares, inner, x_sem, w_sem, c_sem, *, scale, block,
):
    width, columns = w_ref.shape
    blocks = columns // block
    first, second = order[0], order[1]

    def x_copy(at, chosen):
        return pltpu.make_async_copy(x_hbm.at[chosen], x_ref.at[at], x_sem.at[at])

    def c_copy(at):
        part = pl.ds(pl.multiple_of(at * block, block), block)
        return pltpu.make_async_copy(c_hbm.at[first, :, part], c_ref.at[0, :, part], c_sem.at[at])

    def w_copy(at):
        part = pl.ds(pl.multiple_of(at * block, block), block)
        return pltpu.make_async_copy(w_hbm.at[:, part], w_ref.at[:, part], w_sem.at[at])

    later = pltpu.make_async_copy(c_hbm.at[second], c_ref.at[1], c_sem.at[blocks])
    x_copy(0, first).start()
    for at in range(min(AHEAD, blocks)):
        w_copy(at).start()
        c_copy(at).start()
    squares[...] = jnp.zeros_like(squares)
    inner[...] = jnp.zeros_like(inner)
    piece = width // blocks // 128 * 128
    x_copy(0, first).wait()

    def one(at, carry):
        @pl.when(at + AHEAD < blocks)
        def _():
            w_copy(at + AHEAD).start()
            c_copy(at + AHEAD).start()

        @pl.when(at + AHEAD == blocks)
        def _():
            x_copy(1, second).start()
            later.start()

        w_copy(at).wait()
        c_copy(at).wait()
        part = pl.ds(pl.multiple_of(at * block, block), block)
        hidden = jnp.dot(x_ref[0], w_ref[:, part], preferred_element_type=F32) * scale
        h_ref[:, part] = hidden
        target = c_ref[0, :, part].astype(F32)
        squares[...] += lane_fold(hidden * hidden)
        inner[...] += lane_fold(target * hidden)
        flip = pl.ds(pl.multiple_of(at * piece, 128), piece)
        xt_ref[flip, :] = x_ref[0, :, flip].T
        return carry

    lax.fori_loop(0, blocks, one, 0)
    if blocks < AHEAD:
        x_copy(1, second).start()
        later.start()
    if piece * blocks < width:
        xt_ref[piece * blocks :, :] = x_ref[0, :, piece * blocks :].T
    write_stats(stats_ref, squares, inner)
    x_copy(1, second).wait()
    later.wait()


def forward(order, tokens, weight, target):
    steps, count, width = tokens.shape
    columns = weight.shape[1]
    block = width_block(columns)
    blocks = columns // block
    whole = pl.BlockSpec(memory_space=pltpu.VMEM)
    return pl.pallas_call(
        functools.partial(forward_kernel, scale=width**-0.5, block=block),
        out_shape=(
            pltpu.VMEM((count, columns), F32),
            pltpu.VMEM((width, count), BF16),
            jax.ShapeDtypeStruct((2, count), F32),
            pltpu.VMEM(tokens.shape, BF16),
            pltpu.VMEM(weight.shape, BF16),
            pltpu.VMEM(target.shape, BF16),
        ),
        in_specs=[pl.BlockSpec(memory_space=pltpu.SMEM)] + [pl.BlockSpec(memory_space=pl.ANY)] * 3,
        out_specs=(whole,) * 6,
        scratch_shapes=[
            pltpu.VMEM((count, 128), F32),
            pltpu.VMEM((count, 128), F32),
            pltpu.SemaphoreType.DMA((steps,)),
            pltpu.SemaphoreType.DMA((blocks,)),
            pltpu.SemaphoreType.DMA((blocks + 1,)),
        ],
        compiler_params=pltpu.CompilerParams(vmem_limit_bytes=KERNEL_VMEM),
        name="forward_first",
    )(order, tokens, weight, target)


def middle_kernel(
    parts, xt_ref, x_ref, w_ref, h_ref, c_ref,
    g_ref, h2_ref, xt2_ref, stats_ref, loss_ref,
    by_target, by_hidden, even, odd, squares, inner, *, scale, units, rows, block,
):
    count, columns = h_ref.shape
    width = w_ref.shape[0]
    blocks = columns // block
    factors, loss = token_factors(tree_sum([part[...] for part in parts]), units, count)
    by_target[...] = spread(factors[:, 0:1], block)
    by_hidden[...] = spread(factors[:, 1:2], block)
    loss_ref[...] = jnp.broadcast_to(loss, loss_ref.shape)
    squares[...] = jnp.zeros_like(squares)
    inner[...] = jnp.zeros_like(inner)
    piece = width // blocks // 128 * 128
    keep = 1.0 - learn_rate * decay_rate

    def span(at):
        return pl.ds(pl.multiple_of(at * block, block), block)

    def update(at, current):
        cols = span(at)
        grad_rows = (
            c_ref[0, :, cols].astype(F32) * by_target[...] - h_ref[:, cols] * by_hidden[...]
        ).astype(BF16)
        for low in range(0, width, rows):
            part = pl.ds(low, rows)
            product = jnp.dot(xt_ref[part, :], grad_rows, preferred_element_type=F32)
            g_ref[part, cols] = product.astype(BF16)
            moved = product / (jnp.abs(product) + adam_eps / scale)
            current[part, :] = (
                keep * w_ref[part, cols].astype(F32) - learn_rate * moved
            ).astype(BF16)
        flip = pl.ds(pl.multiple_of(at * piece, 128), piece)
        xt2_ref[flip, :] = x_ref[1, :, flip].T

    def project(at, current):
        cols = span(at)
        hidden = jnp.dot(x_ref[1], current[...], preferred_element_type=F32) * scale
        h2_ref[:, cols] = hidden
        squares[...] += lane_fold(hidden * hidden)
        inner[...] += lane_fold(c_ref[1, :, cols].astype(F32) * hidden)

    def pair(at, carry):
        update(2 * at + 1, odd)
        project(2 * at, even)
        update(2 * at + 2, even)
        project(2 * at + 1, odd)
        return carry

    update(0, even)
    lax.fori_loop(0, (blocks - 1) // 2, pair, 0)
    if blocks % 2:
        project(blocks - 1, even)
    else:
        update(blocks - 1, odd)
        project(blocks - 2, even)
        project(blocks - 1, odd)
    if piece * blocks < width:
        xt2_ref[piece * blocks :, :] = x_ref[1, :, piece * blocks :].T
    write_stats(stats_ref, squares, inner)


def middle(stats, flipped, tokens, weight, hidden, target, units):
    _, count, width = tokens.shape
    columns = weight.shape[1]
    block = width_block(columns)
    whole = pl.BlockSpec(memory_space=pltpu.VMEM)
    return pl.pallas_call(
        functools.partial(
            middle_kernel, scale=width**-0.5, units=units, rows=min(ROWS, width), block=block
        ),
        out_shape=(
            pltpu.VMEM((width, columns), BF16),
            pltpu.VMEM((count, columns), F32),
            pltpu.VMEM((width, count), BF16),
            jax.ShapeDtypeStruct((2, count), F32),
            jax.ShapeDtypeStruct((1, 128), F32),
        ),
        in_specs=[[whole] * len(stats)] + [whole] * 5,
        out_specs=(whole,) * 5,
        scratch_shapes=[
            pltpu.VMEM((count, block), F32),
            pltpu.VMEM((count, block), F32),
            pltpu.VMEM((width, block), BF16),
            pltpu.VMEM((width, block), BF16),
            pltpu.VMEM((count, 128), F32),
            pltpu.VMEM((count, 128), F32),
        ],
        compiler_params=pltpu.CompilerParams(vmem_limit_bytes=KERNEL_VMEM),
        name="middle",
    )(stats, flipped, tokens, weight, hidden, target)


def factors_kernel(*refs, units):
    parts, (by_target, by_hidden, loss_ref) = refs[:-3], refs[-3:]
    count = by_target.shape[0]
    factors, loss = token_factors(tree_sum([part[...] for part in parts]), units, count)
    by_target[...] = spread(factors[:, 0:1], LANES)
    by_hidden[...] = spread(factors[:, 1:2], LANES)
    loss_ref[...] = jnp.broadcast_to(loss, loss_ref.shape)


def last_part(
    by_target, by_hidden, xt_ref, w_ref, g_ref, h_ref, c_ref, final_ref, grad_rows,
    *, scale, low, block, rows,
):
    count = h_ref.shape[0]
    cols = slice(low, low + block)

    def prepare(at, carry):
        part = pl.ds(pl.multiple_of(at * TOKEN_ROWS, TOKEN_ROWS), TOKEN_ROWS)
        for lane in range(0, block, LANES):
            here = slice(low + lane, low + lane + LANES)
            grad_rows[part, lane : lane + LANES] = (
                c_ref[1, part, here].astype(F32) * by_target[part, :]
                - h_ref[part, here] * by_hidden[part, :]
            ).astype(BF16)
        return carry

    lax.fori_loop(0, count // TOKEN_ROWS, prepare, 0)
    bias_first = 1.0 - beta_first**2
    bias_second = 1.0 - beta_second**2
    old_moment = learn_rate * scale * beta_first * (1.0 - beta_first) / bias_first
    new_moment = learn_rate * scale * (1.0 - beta_first) / bias_first
    old_second = scale * scale * beta_second * (1.0 - beta_second) / bias_second
    new_second = scale * scale * (1.0 - beta_second) / bias_second
    keep = 1.0 - learn_rate * decay_rate

    def one(at, carry):
        part = pl.ds(pl.multiple_of(at * rows, rows), rows)
        product = jnp.dot(xt_ref[part, :], grad_rows[...], preferred_element_type=F32)
        first = g_ref[part, cols].astype(F32)
        moved = first / (jnp.abs(first) + adam_eps / scale)
        moment = old_moment * first + new_moment * product
        second = old_second * (first * first) + new_second * (product * product)
        second = jnp.maximum(second, tiny_square)
        fresh = moment / (second * lax.rsqrt(second) + adam_eps)
        master = keep * keep * w_ref[part, cols].astype(F32)
        final_ref[part, :] = (master - (keep * learn_rate * moved + fresh)).astype(BF16)
        return carry

    lax.fori_loop(0, xt_ref.shape[0] // rows, one, 0)


def first_piece_kernel(*refs, units, parts, **sizes):
    stats, operands, outs, grad_rows = refs[:parts], refs[parts:-5], refs[-5:-1], refs[-1]
    final_ref, by_target, by_hidden, loss_ref = outs
    factors_kernel(*stats, by_target, by_hidden, loss_ref, units=units)
    last_part(by_target, by_hidden, *operands, final_ref, grad_rows, **sizes)


def piece_call(kernel, outs, operands, width, count, block):
    whole = pl.BlockSpec(memory_space=pltpu.VMEM)
    return pl.pallas_call(
        kernel,
        out_shape=outs,
        in_specs=[whole] * len(operands),
        out_specs=jax.tree.map(lambda _: whole, outs),
        scratch_shapes=[pltpu.VMEM((count, block), BF16)],
        compiler_params=pltpu.CompilerParams(vmem_limit_bytes=KERNEL_VMEM),
        cost_estimate=pl.CostEstimate(
            flops=2 * width * count * block,
            bytes_accessed=2 * width * (3 * block + count) + 6 * count * block,
            transcendentals=3 * width * block,
        ),
    )(*operands)


def first_piece(stats, operands, units, low, block):
    width, count = operands[0].shape
    rows = min(PIECE_CELLS // block, width)
    kernel = functools.partial(
        first_piece_kernel, units=units, parts=len(stats), scale=width**-0.5, low=low, block=block, rows=rows
    )
    outs = (
        pltpu.VMEM((width, block), BF16),
        pltpu.VMEM((count, LANES), F32),
        pltpu.VMEM((count, LANES), F32),
        jax.ShapeDtypeStruct((1, LANES), F32),
    )
    return piece_call(kernel, outs, (*stats, *operands), width, count, block)


def next_piece(factors, operands, low, block):
    width, count = operands[0].shape
    rows = min(PIECE_CELLS // block, width)
    kernel = functools.partial(last_part, scale=width**-0.5, low=low, block=block, rows=rows)
    outs = pltpu.VMEM((width, block), BF16)
    return piece_call(kernel, outs, (*factors, *operands), width, count, block)


def mean_kernel(own_ref, peer_ref, *refs, low, parts):
    out_ref, buffer, sems = refs[-3:]
    width, block = own_ref.shape
    rows = width // parts
    step = min(MEAN_CELLS // block, rows)

    def copy(at):
        part = pl.ds(pl.multiple_of(at * rows, rows), rows)
        return pltpu.make_async_copy(
            buffer.at[part, :], out_ref.at[part, low : low + block], sems.at[at]
        )

    def one(at, carry):
        def inner(sub, carry):
            part = pl.ds(pl.multiple_of(at * rows + sub * step, step), step)
            buffer[part, :] = (
                (own_ref[part, :].astype(F32) + peer_ref[part, :].astype(F32)) * 0.5
            ).astype(BF16)
            return carry

        lax.fori_loop(0, rows // step, inner, 0)
        copy(at).start()
        return carry

    lax.fori_loop(0, parts, one, 0)
    for at in range(parts):
        copy(at).wait()


def mean_into(out, own, peer, columns, low):
    width, block = own.shape
    parts = 4 if width % 512 == 0 else 1
    whole = pl.BlockSpec(memory_space=pltpu.VMEM)
    anywhere = pl.BlockSpec(memory_space=pl.ANY)
    return pl.pallas_call(
        functools.partial(mean_kernel, low=low, parts=parts),
        out_shape=jax.ShapeDtypeStruct((width, columns), BF16),
        in_specs=[whole, whole] + ([] if out is None else [anywhere]),
        out_specs=anywhere,
        scratch_shapes=[
            pltpu.VMEM((width, block), BF16),
            pltpu.SemaphoreType.DMA((parts,)),
        ],
        input_output_aliases={} if out is None else {2: 0},
        compiler_params=pltpu.CompilerParams(vmem_limit_bytes=KERNEL_VMEM),
        cost_estimate=pl.CostEstimate(
            flops=2 * width * block, bytes_accessed=6 * width * block, transcendentals=0
        ),
        name="mean",
    )(*([own, peer] + ([] if out is None else [out])))


def tree_sum(parts):
    while len(parts) > 1:
        parts = [parts[at] + parts[at + 1] for at in range(0, len(parts), 2)]
    return parts[0]


def everyones(array, axis):
    devices = lax.axis_size(axis)
    if devices & (devices - 1):
        return [lax.psum(array, axis)]
    return [array] + [
        lax.ppermute(array, axis, [(i, i ^ flip) for i in range(devices)])
        for flip in range(1, devices)
    ]


def shifted(array, axis, by):
    devices = lax.axis_size(axis)
    return lax.ppermute(array, axis, [(i, (i + by) % devices) for i in range(devices)])


def shards(weight, tokens, cotangent, batch_order, step_index):
    weight, tokens, target, order = weight[0], tokens[0], cotangent[0], batch_order[0]
    _, columns = weight.shape
    units = columns * lax.axis_size("tp")
    levels = lax.axis_size("rep").bit_length() - 1
    hop_level = step_index[0] % levels

    pieces = chunks_of(columns)

    def chain(exponent):
        def run(order, tokens, weight, target):
            hidden, flipped, stats, tokens, weight, target = forward(order, tokens, weight, target)
            stats = everyones(stats, "tp")
            gradient, hidden, flipped, stats, loss_first = middle(
                stats, flipped, tokens, weight, hidden, target, units
            )
            stats = everyones(stats, "tp")
            finals, peers = [], []
            operands = (flipped, weight, gradient, hidden, target)
            for at, (low, size) in enumerate(pieces):
                if at == 0:
                    final, *factors, loss_second = first_piece(stats, operands, units, low, size)
                else:
                    final = next_piece(factors, operands, low, size)
                finals.append(final)
                peers.append(shifted(final, "rep", 2**exponent))
            out = None
            for (low, _), final, peer in zip(pieces, finals, peers):
                out = mean_into(out, final, peer, columns, low)
            return out, jnp.concatenate([loss_first[:, :1], loss_second[:, :1]], axis=1)

        return run

    averaged, losses = lax.switch(
        hop_level, [chain(exponent) for exponent in range(levels)], order, tokens, weight, target
    )
    return (averaged[None], losses)


def solution(mesh):
    placed = (
        P("rep", None, "tp"),
        P("rep", None, None, None),
        P("rep", None, None, "tp"),
        P("rep", None),
        P(),
    )
    return jax.shard_map(
        shards,
        mesh=mesh,
        in_specs=placed,
        out_specs=(P("rep", None, "tp"), P("rep", None)),
        check_vma=False,
    )
```

```python
import functools

import jax
import jax.numpy as jnp
from jax import lax
from jax.experimental import pallas as pl
from jax.experimental.pallas import tpu as pltpu
from jax.sharding import PartitionSpec as P


beta_first = 0.9
beta_second = 0.95
learn_rate = 0.05
decay_rate = 0.1
adam_eps = 1e-05
norm_eps = 1e-06
tiny_square = 1e-30

F32 = jnp.float32
BF16 = jnp.bfloat16
KERNEL_VMEM = 16 * 1024 * 1024
ROWS = 256
LANES = 128
TOKEN_ROWS = 64
PIECE_CELLS = 256 * 256
MEAN_CELLS = 128 * 256
PIECE_COLUMNS = 512
AHEAD = 3


def width_block(columns):
    for block in (256, 128):
        if columns % block == 0:
            return block
    return columns


def chunks_of(width, columns):
    if columns % LANES or columns <= 2 * LANES or width % (4 * LANES):
        return [(slice(0, width), slice(0, columns))]
    halves = (slice(0, width // 2), slice(width // 2, width))
    pieces = [(half, slice(0, LANES)) for half in halves]
    low = LANES
    while low < columns - LANES:
        high = min(low + PIECE_COLUMNS, columns - LANES)
        pieces.append((slice(0, width), slice(low, high)))
        low = high
    return pieces + [(half, slice(low, columns)) for half in halves]


def lane_fold(values):
    total = values[:, :128]
    for at in range(128, values.shape[1], 128):
        total = total + values[:, at : at + 128]
    return total


def write_stats(stats_ref, squares, inner):
    stats_ref[0:1, :] = jnp.sum(squares[...].T, axis=0, keepdims=True)
    stats_ref[1:2, :] = jnp.sum(inner[...].T, axis=0, keepdims=True)


def token_factors(stats, units, tokens, scale):
    squares, inner = stats[0:1, :] * (scale * scale), stats[1:2, :] * scale
    radius = jnp.sqrt(squares / units + norm_eps)
    loss = jnp.sum(inner / radius, axis=1, keepdims=True) / tokens
    by_target = 1.0 / (radius * tokens)
    by_hidden = scale * inner / (units * radius * radius * radius * tokens)
    pad = jnp.zeros((6, stats.shape[1]), F32)
    columns = jnp.concatenate([by_target, by_hidden, pad], axis=0).T
    return columns, loss


def spread(column, lanes):
    return jnp.broadcast_to(column, (column.shape[0], lanes))


def in_hbm(array):
    return pltpu.with_memory_space_constraint(array, pltpu.HBM)


def forward_kernel(
    order_hbm, x_hbm, w_hbm, c_hbm, h_ref, xt_ref, stats_ref, x_ref, w_ref, c_ref,
    order, squares, inner, order_sem, x_sem, w_sem, c_sem, *, block,
):
    width, columns = w_ref.shape
    blocks = columns // block
    order_copy = pltpu.make_async_copy(order_hbm, order, order_sem)
    order_copy.start()

    def w_copy(at):
        part = pl.ds(pl.multiple_of(at * block, block), block)
        return pltpu.make_async_copy(w_hbm.at[:, part], w_ref.at[:, part], w_sem.at[at])

    w_copy(0).start()
    squares[...] = jnp.zeros_like(squares)
    inner[...] = jnp.zeros_like(inner)
    piece = width // blocks // 128 * 128
    order_copy.wait()
    first, second = order[0], order[1]

    def x_copy(at, chosen):
        return pltpu.make_async_copy(x_hbm.at[chosen], x_ref.at[at], x_sem.at[at])

    def c_copy(at):
        part = pl.ds(pl.multiple_of(at * block, block), block)
        return pltpu.make_async_copy(c_hbm.at[first, :, part], c_ref.at[0, :, part], c_sem.at[at])

    later = pltpu.make_async_copy(c_hbm.at[second], c_ref.at[1], c_sem.at[blocks])
    x_copy(0, first).start()
    c_copy(0).start()
    for at in range(1, min(AHEAD, blocks)):
        w_copy(at).start()
        c_copy(at).start()
    x_copy(0, first).wait()

    def one(at, carry):
        @pl.when(at + AHEAD < blocks)
        def _():
            w_copy(at + AHEAD).start()
            c_copy(at + AHEAD).start()

        @pl.when(at + AHEAD == blocks)
        def _():
            x_copy(1, second).start()
            later.start()

        w_copy(at).wait()
        c_copy(at).wait()
        part = pl.ds(pl.multiple_of(at * block, block), block)
        hidden = jnp.dot(x_ref[0], w_ref[:, part], preferred_element_type=F32)
        h_ref[:, part] = hidden
        target = c_ref[0, :, part].astype(F32)
        squares[...] += lane_fold(hidden * hidden)
        inner[...] += lane_fold(target * hidden)
        flip = pl.ds(pl.multiple_of(at * piece, 128), piece)
        xt_ref[flip, :] = x_ref[0, :, flip].T
        return carry

    lax.fori_loop(0, blocks, one, 0)
    if blocks < AHEAD:
        x_copy(1, second).start()
        later.start()
    if piece * blocks < width:
        xt_ref[piece * blocks :, :] = x_ref[0, :, piece * blocks :].T
    write_stats(stats_ref, squares, inner)
    x_copy(1, second).wait()
    later.wait()


def forward(order, tokens, weight, target):
    steps, count, width = tokens.shape
    columns = weight.shape[1]
    block = width_block(columns)
    blocks = columns // block
    whole = pl.BlockSpec(memory_space=pltpu.VMEM)
    return pl.pallas_call(
        functools.partial(forward_kernel, block=block),
        out_shape=(
            pltpu.VMEM((count, columns), F32),
            pltpu.VMEM((width, count), BF16),
            jax.ShapeDtypeStruct((2, count), F32),
            pltpu.VMEM(tokens.shape, BF16),
            pltpu.VMEM(weight.shape, BF16),
            pltpu.VMEM(target.shape, BF16),
        ),
        in_specs=[pl.BlockSpec(memory_space=pl.ANY)] * 4,
        out_specs=(whole,) * 6,
        scratch_shapes=[
            pltpu.SMEM(order.shape, order.dtype),
            pltpu.VMEM((count, 128), F32),
            pltpu.VMEM((count, 128), F32),
            pltpu.SemaphoreType.DMA(()),
            pltpu.SemaphoreType.DMA((steps,)),
            pltpu.SemaphoreType.DMA((blocks,)),
            pltpu.SemaphoreType.DMA((blocks + 1,)),
        ],
        compiler_params=pltpu.CompilerParams(vmem_limit_bytes=KERNEL_VMEM),
        name="forward_first",
    )(in_hbm(order), in_hbm(tokens), in_hbm(weight), in_hbm(target))


def middle_kernel(
    parts, xt_ref, x_ref, w_ref, h_ref, c_ref,
    g_ref, h2_ref, xt2_ref, stats_ref, loss_ref,
    by_target, by_hidden, even, odd, squares, inner, *, scale, units, rows, block,
):
    count, columns = h_ref.shape
    width = w_ref.shape[0]
    blocks = columns // block
    factors, loss = token_factors(tree_sum([part[...] for part in parts]), units, count, scale)
    by_target[...] = spread(factors[:, 0:1], block)
    by_hidden[...] = spread(factors[:, 1:2], block)
    loss_ref[...] = jnp.broadcast_to(loss, loss_ref.shape)
    squares[...] = jnp.zeros_like(squares)
    inner[...] = jnp.zeros_like(inner)
    piece = width // blocks // 128 * 128
    keep = 1.0 - learn_rate * decay_rate

    def span(at):
        return pl.ds(pl.multiple_of(at * block, block), block)

    def update(at, current):
        cols = span(at)
        grad_rows = (
            c_ref[0, :, cols].astype(F32) * by_target[...] - h_ref[:, cols] * by_hidden[...]
        ).astype(BF16)
        for low in range(0, width, rows):
            part = pl.ds(low, rows)
            product = jnp.dot(xt_ref[part, :], grad_rows, preferred_element_type=F32)
            g_ref[part, cols] = product.astype(BF16)
            moved = product / (jnp.abs(product) + adam_eps / scale)
            current[part, :] = (
                keep * w_ref[part, cols].astype(F32) - learn_rate * moved
            ).astype(BF16)
        flip = pl.ds(pl.multiple_of(at * piece, 128), piece)
        xt2_ref[flip, :] = x_ref[1, :, flip].T

    def project(at, current):
        cols = span(at)
        hidden = jnp.dot(x_ref[1], current[...], preferred_element_type=F32)
        h2_ref[:, cols] = hidden
        squares[...] += lane_fold(hidden * hidden)
        inner[...] += lane_fold(c_ref[1, :, cols].astype(F32) * hidden)

    def pair(at, carry):
        update(2 * at + 1, odd)
        project(2 * at, even)
        update(2 * at + 2, even)
        project(2 * at + 1, odd)
        return carry

    update(0, even)
    lax.fori_loop(0, (blocks - 1) // 2, pair, 0)
    if blocks % 2:
        project(blocks - 1, even)
    else:
        update(blocks - 1, odd)
        project(blocks - 2, even)
        project(blocks - 1, odd)
    if piece * blocks < width:
        xt2_ref[piece * blocks :, :] = x_ref[1, :, piece * blocks :].T
    write_stats(stats_ref, squares, inner)


def middle(stats, flipped, tokens, weight, hidden, target, units):
    _, count, width = tokens.shape
    columns = weight.shape[1]
    block = width_block(columns)
    whole = pl.BlockSpec(memory_space=pltpu.VMEM)
    return pl.pallas_call(
        functools.partial(
            middle_kernel, scale=width**-0.5, units=units, rows=min(ROWS, width), block=block
        ),
        out_shape=(
            pltpu.VMEM((width, columns), BF16),
            pltpu.VMEM((count, columns), F32),
            pltpu.VMEM((width, count), BF16),
            jax.ShapeDtypeStruct((2, count), F32),
            jax.ShapeDtypeStruct((1, 128), F32),
        ),
        in_specs=[[whole] * len(stats)] + [whole] * 5,
        out_specs=(whole,) * 5,
        scratch_shapes=[
            pltpu.VMEM((count, block), F32),
            pltpu.VMEM((count, block), F32),
            pltpu.VMEM((width, block), BF16),
            pltpu.VMEM((width, block), BF16),
            pltpu.VMEM((count, 128), F32),
            pltpu.VMEM((count, 128), F32),
        ],
        compiler_params=pltpu.CompilerParams(vmem_limit_bytes=KERNEL_VMEM),
        name="middle",
    )(stats, flipped, tokens, weight, hidden, target)


def factors_kernel(*refs, units, scale):
    parts, (by_target, by_hidden, loss_ref) = refs[:-3], refs[-3:]
    count = by_target.shape[0]
    factors, loss = token_factors(tree_sum([part[...] for part in parts]), units, count, scale)
    by_target[...] = spread(factors[:, 0:1], LANES)
    by_hidden[...] = spread(factors[:, 1:2], LANES)
    loss_ref[...] = jnp.broadcast_to(loss, loss_ref.shape)


def last_part(
    by_target, by_hidden, xt_ref, w_ref, g_ref, h_ref, c_ref, final_ref, grad_rows,
    *, scale, tall, cols, rows,
):
    count = h_ref.shape[0]
    low, block = cols.start, cols.stop - cols.start

    def prepare(at, carry):
        part = pl.ds(pl.multiple_of(at * TOKEN_ROWS, TOKEN_ROWS), TOKEN_ROWS)
        for lane in range(0, block, LANES):
            here = slice(low + lane, low + lane + LANES)
            grad_rows[part, lane : lane + LANES] = (
                c_ref[1, part, here].astype(F32) * by_target[part, :]
                - h_ref[part, here] * by_hidden[part, :]
            ).astype(BF16)
        return carry

    lax.fori_loop(0, count // TOKEN_ROWS, prepare, 0)
    bias_first = 1.0 - beta_first**2
    bias_second = 1.0 - beta_second**2
    old_moment = learn_rate * scale * beta_first * (1.0 - beta_first) / bias_first
    new_moment = learn_rate * scale * (1.0 - beta_first) / bias_first
    old_second = scale * scale * beta_second * (1.0 - beta_second) / bias_second
    new_second = scale * scale * (1.0 - beta_second) / bias_second
    keep = 1.0 - learn_rate * decay_rate

    def one(at, carry):
        here = pl.ds(pl.multiple_of(at * rows, rows), rows)
        part = pl.ds(pl.multiple_of(tall.start + at * rows, rows), rows)
        product = jnp.dot(xt_ref[part, :], grad_rows[...], preferred_element_type=F32)
        first = g_ref[part, cols].astype(F32)
        moved = first / (jnp.abs(first) + adam_eps / scale)
        moment = old_moment * first + new_moment * product
        second = old_second * (first * first) + new_second * (product * product)
        second = jnp.maximum(second, tiny_square)
        fresh = moment / (second * lax.rsqrt(second) + adam_eps)
        master = keep * keep * w_ref[part, cols].astype(F32)
        final_ref[here, :] = (master - (keep * learn_rate * moved + fresh)).astype(BF16)
        return carry

    lax.fori_loop(0, final_ref.shape[0] // rows, one, 0)


def first_piece_kernel(*refs, units, parts, scale, **sizes):
    stats, operands, outs, grad_rows = refs[:parts], refs[parts:-5], refs[-5:-1], refs[-1]
    final_ref, by_target, by_hidden, loss_ref = outs
    factors_kernel(*stats, by_target, by_hidden, loss_ref, units=units, scale=scale)
    last_part(by_target, by_hidden, *operands, final_ref, grad_rows, scale=scale, **sizes)


def piece_call(kernel, outs, operands, tall, cols, count, units):
    whole = pl.BlockSpec(memory_space=pltpu.VMEM)
    height, block = tall.stop - tall.start, cols.stop - cols.start
    width = operands[-4].shape[0]
    return pl.pallas_call(
        functools.partial(
            kernel, scale=width**-0.5, tall=tall, cols=cols, rows=min(PIECE_CELLS // block, height), **units
        ),
        out_shape=(pltpu.VMEM((height, block), BF16), *outs),
        in_specs=[whole] * len(operands),
        out_specs=(whole,) * (1 + len(outs)),
        scratch_shapes=[pltpu.VMEM((count, block), BF16)],
        compiler_params=pltpu.CompilerParams(vmem_limit_bytes=KERNEL_VMEM),
        cost_estimate=pl.CostEstimate(
            flops=2 * height * count * block,
            bytes_accessed=2 * height * (3 * block + count) + 6 * count * block,
            transcendentals=3 * height * block,
        ),
    )(*operands)


def first_piece(stats, operands, units, tall, cols):
    count = operands[0].shape[1]
    outs = (
        pltpu.VMEM((count, LANES), F32),
        pltpu.VMEM((count, LANES), F32),
        jax.ShapeDtypeStruct((1, LANES), F32),
    )
    extra = {"units": units, "parts": len(stats)}
    return piece_call(first_piece_kernel, outs, (*stats, *operands), tall, cols, count, extra)


def next_piece(factors, operands, tall, cols):
    count = operands[0].shape[1]
    return piece_call(last_part, (), (*factors, *operands), tall, cols, count, {})[0]


def losses_kernel(first_ref, second_ref, out_ref, buffer, sem):
    buffer[:, 0:1] = first_ref[:, 0:1]
    buffer[:, 1:2] = second_ref[:, 0:1]
    copy = pltpu.make_async_copy(buffer, out_ref, sem)
    copy.start()
    copy.wait()


def losses_out(first, second):
    whole = pl.BlockSpec(memory_space=pltpu.VMEM)
    return pl.pallas_call(
        losses_kernel,
        out_shape=pltpu.HBM((1, 2), F32),
        in_specs=[whole, whole],
        out_specs=pl.BlockSpec(memory_space=pl.ANY),
        scratch_shapes=[pltpu.VMEM((1, 2), F32), pltpu.SemaphoreType.DMA(())],
        compiler_params=pltpu.CompilerParams(vmem_limit_bytes=KERNEL_VMEM),
        name="losses",
    )(first, second)


def mean_kernel(own_ref, peer_ref, *refs, tall, cols, parts):
    out_ref, buffer, sems = refs[-3:]
    height, block = own_ref.shape
    rows = height // parts
    step = min(MEAN_CELLS // block, rows)

    def copy(at):
        part = pl.ds(pl.multiple_of(at * rows, rows), rows)
        there = pl.ds(pl.multiple_of(tall.start + at * rows, rows), rows)
        return pltpu.make_async_copy(buffer.at[part, :], out_ref.at[there, cols], sems.at[at])

    def one(at, carry):
        def inner(sub, carry):
            part = pl.ds(pl.multiple_of(at * rows + sub * step, step), step)
            buffer[part, :] = (
                (own_ref[part, :].astype(F32) + peer_ref[part, :].astype(F32)) * 0.5
            ).astype(BF16)
            return carry

        lax.fori_loop(0, rows // step, inner, 0)
        copy(at).start()
        return carry

    lax.fori_loop(0, parts, one, 0)
    for at in range(parts):
        copy(at).wait()


def mean_into(out, own, peer, shape, tall, cols):
    height, block = own.shape
    parts = 4 if height % (4 * LANES) == 0 else 1
    whole = pl.BlockSpec(memory_space=pltpu.VMEM)
    anywhere = pl.BlockSpec(memory_space=pl.ANY)
    return pl.pallas_call(
        functools.partial(mean_kernel, tall=tall, cols=cols, parts=parts),
        out_shape=jax.ShapeDtypeStruct(shape, BF16),
        in_specs=[whole, whole] + ([] if out is None else [anywhere]),
        out_specs=anywhere,
        scratch_shapes=[
            pltpu.VMEM((height, block), BF16),
            pltpu.SemaphoreType.DMA((parts,)),
        ],
        input_output_aliases={} if out is None else {2: 0},
        compiler_params=pltpu.CompilerParams(vmem_limit_bytes=KERNEL_VMEM),
        cost_estimate=pl.CostEstimate(
            flops=2 * height * block, bytes_accessed=6 * height * block, transcendentals=0
        ),
        name="mean",
    )(*([own, peer] + ([] if out is None else [out])))


def tree_sum(parts):
    while len(parts) > 1:
        parts = [parts[at] + parts[at + 1] for at in range(0, len(parts), 2)]
    return parts[0]


def everyones(array, axis):
    devices = lax.axis_size(axis)
    if devices & (devices - 1):
        return [lax.psum(array, axis)]
    return [array] + [
        lax.ppermute(array, axis, [(i, i ^ flip) for i in range(devices)])
        for flip in range(1, devices)
    ]


def shifted(array, axis, by):
    devices = lax.axis_size(axis)
    return lax.ppermute(array, axis, [(i, (i + by) % devices) for i in range(devices)])


def shards(weight, tokens, cotangent, batch_order, step_index):
    weight, tokens, target, order = weight[0], tokens[0], cotangent[0], batch_order[0]
    width, columns = weight.shape
    units = columns * lax.axis_size("tp")
    levels = lax.axis_size("rep").bit_length() - 1
    hop_level = step_index[0] % levels

    pieces = chunks_of(width, columns)

    def chain(exponent):
        def run(order, tokens, weight, target):
            hidden, flipped, stats, tokens, weight, target = forward(order, tokens, weight, target)
            stats = everyones(stats, "tp")
            gradient, hidden, flipped, stats, loss_first = middle(
                stats, flipped, tokens, weight, hidden, target, units
            )
            stats = everyones(stats, "tp")
            finals, peers = [], []
            operands = (flipped, weight, gradient, hidden, target)
            for at, piece in enumerate(pieces):
                if at == 0:
                    final, *factors, loss_second = first_piece(stats, operands, units, *piece)
                else:
                    final = next_piece(factors, operands, *piece)
                finals.append(final)
                peers.append(shifted(final, "rep", 2**exponent))
            out = None
            for piece, final, peer in zip(pieces, finals, peers):
                out = mean_into(out, final, peer, weight.shape, *piece)
            return out, losses_out(loss_first, loss_second)

        return run

    averaged, losses = lax.switch(
        hop_level, [chain(exponent) for exponent in range(levels)], order, tokens, weight, target
    )
    return (averaged[None], losses)


def solution(mesh):
    placed = (
        P("rep", None, "tp"),
        P("rep", None, None, None),
        P("rep", None, None, "tp"),
        P("rep", None),
        P(),
    )
    return jax.shard_map(
        shards,
        mesh=mesh,
        in_specs=placed,
        out_specs=(P("rep", None, "tp"), P("rep", None)),
        check_vma=False,
    )
```

```python
import functools

import jax
import jax.numpy as jnp
from jax import lax
from jax.experimental import pallas as pl
from jax.experimental.pallas import tpu as pltpu
from jax.sharding import PartitionSpec as P


beta_first = 0.9
beta_second = 0.95
learn_rate = 0.05
decay_rate = 0.1
adam_eps = 1e-05
norm_eps = 1e-06
tiny_square = 1e-30

F32 = jnp.float32
BF16 = jnp.bfloat16
KERNEL_VMEM = 16 * 1024 * 1024
ROWS = 256
LANES = 128
TOKEN_ROWS = 64
PIECE_CELLS = 256 * 256
MEAN_CELLS = 128 * 256
PIECE_COLUMNS = 512
AHEAD = 3


def width_block(columns):
    for block in (256, 128):
        if columns % block == 0:
            return block
    return columns


def chunks_of(width, columns):
    if columns % LANES or columns <= 2 * LANES or width % (4 * LANES):
        return [(slice(0, width), slice(0, columns))]
    halves = (slice(0, width // 2), slice(width // 2, width))
    pieces = [(half, slice(0, LANES)) for half in halves]
    low = LANES
    while low < columns - LANES:
        high = min(low + PIECE_COLUMNS, columns - LANES)
        pieces.append((slice(0, width), slice(low, high)))
        low = high
    return pieces + [(half, slice(low, columns)) for half in halves]


def lane_fold(values):
    total = values[:, :128]
    for at in range(128, values.shape[1], 128):
        total = total + values[:, at : at + 128]
    return total


def write_stats(stats_ref, squares, inner):
    stats_ref[0:1, :] = jnp.sum(squares[...].T, axis=0, keepdims=True)
    stats_ref[1:2, :] = jnp.sum(inner[...].T, axis=0, keepdims=True)


def token_factors(stats, units, tokens, scale):
    squares, inner = stats[0:1, :] * (scale * scale), stats[1:2, :] * scale
    radius = jnp.sqrt(squares / units + norm_eps)
    loss = jnp.sum(inner / radius, axis=1, keepdims=True) / tokens
    by_target = 1.0 / (radius * tokens)
    by_hidden = scale * inner / (units * radius * radius * radius * tokens)
    pad = jnp.zeros((6, stats.shape[1]), F32)
    columns = jnp.concatenate([by_target, by_hidden, pad], axis=0).T
    return columns, loss


def spread(column, lanes):
    return jnp.broadcast_to(column, (column.shape[0], lanes))


def in_hbm(array):
    return pltpu.with_memory_space_constraint(array, pltpu.HBM)


def forward_kernel(
    order_hbm, x_hbm, w_hbm, c_hbm, h_ref, xt_ref, stats_ref, x_ref, w_ref, c_ref,
    order, squares, inner, order_sem, x_sem, w_sem, c_sem, *, block,
):
    width, columns = w_ref.shape
    blocks = columns // block
    order_copy = pltpu.make_async_copy(order_hbm, order, order_sem)
    order_copy.start()

    def w_copy(at):
        part = pl.ds(pl.multiple_of(at * block, block), block)
        return pltpu.make_async_copy(w_hbm.at[:, part], w_ref.at[:, part], w_sem.at[at])

    w_copy(0).start()
    squares[...] = jnp.zeros_like(squares)
    inner[...] = jnp.zeros_like(inner)
    piece = width // blocks // 128 * 128
    order_copy.wait()
    first, second = order[0], order[1]

    def x_copy(at, chosen):
        return pltpu.make_async_copy(x_hbm.at[chosen], x_ref.at[at], x_sem.at[at])

    def c_copy(at):
        part = pl.ds(pl.multiple_of(at * block, block), block)
        return pltpu.make_async_copy(c_hbm.at[first, :, part], c_ref.at[0, :, part], c_sem.at[at])

    later = pltpu.make_async_copy(c_hbm.at[second], c_ref.at[1], c_sem.at[blocks])
    x_copy(0, first).start()
    c_copy(0).start()
    for at in range(1, min(AHEAD, blocks)):
        w_copy(at).start(priority=1)
        c_copy(at).start(priority=1)
    x_copy(0, first).wait()

    def one(at, carry):
        @pl.when(at + AHEAD < blocks)
        def _():
            w_copy(at + AHEAD).start(priority=1)
            c_copy(at + AHEAD).start(priority=1)

        @pl.when(at + AHEAD == blocks)
        def _():
            x_copy(1, second).start(priority=1)
            later.start(priority=1)

        w_copy(at).wait()
        c_copy(at).wait()
        part = pl.ds(pl.multiple_of(at * block, block), block)
        hidden = jnp.dot(x_ref[0], w_ref[:, part], preferred_element_type=F32)
        h_ref[:, part] = hidden
        target = c_ref[0, :, part].astype(F32)
        squares[...] += lane_fold(hidden * hidden)
        inner[...] += lane_fold(target * hidden)
        flip = pl.ds(pl.multiple_of(at * piece, 128), piece)
        xt_ref[flip, :] = x_ref[0, :, flip].T
        return carry

    lax.fori_loop(0, blocks, one, 0)
    if blocks < AHEAD:
        x_copy(1, second).start()
        later.start()
    if piece * blocks < width:
        xt_ref[piece * blocks :, :] = x_ref[0, :, piece * blocks :].T
    write_stats(stats_ref, squares, inner)
    x_copy(1, second).wait()
    later.wait()


def forward(order, tokens, weight, target):
    steps, count, width = tokens.shape
    columns = weight.shape[1]
    block = width_block(columns)
    blocks = columns // block
    whole = pl.BlockSpec(memory_space=pltpu.VMEM)
    return pl.pallas_call(
        functools.partial(forward_kernel, block=block),
        out_shape=(
            pltpu.VMEM((count, columns), F32),
            pltpu.VMEM((width, count), BF16),
            jax.ShapeDtypeStruct((2, count), F32),
            pltpu.VMEM(tokens.shape, BF16),
            pltpu.VMEM(weight.shape, BF16),
            pltpu.VMEM(target.shape, BF16),
        ),
        in_specs=[pl.BlockSpec(memory_space=pl.ANY)] * 4,
        out_specs=(whole,) * 6,
        scratch_shapes=[
            pltpu.SMEM(order.shape, order.dtype),
            pltpu.VMEM((count, 128), F32),
            pltpu.VMEM((count, 128), F32),
            pltpu.SemaphoreType.DMA(()),
            pltpu.SemaphoreType.DMA((steps,)),
            pltpu.SemaphoreType.DMA((blocks,)),
            pltpu.SemaphoreType.DMA((blocks + 1,)),
        ],
        compiler_params=pltpu.CompilerParams(vmem_limit_bytes=KERNEL_VMEM),
        name="forward_first",
    )(in_hbm(order), in_hbm(tokens), in_hbm(weight), in_hbm(target))


def middle_kernel(
    parts, xt_ref, x_ref, w_ref, h_ref, c_ref,
    g_ref, h2_ref, xt2_ref, stats_ref, loss_ref,
    by_target, by_hidden, even, odd, squares, inner, *, scale, units, rows, block,
):
    count, columns = h_ref.shape
    width = w_ref.shape[0]
    blocks = columns // block
    factors, loss = token_factors(tree_sum([part[...] for part in parts]), units, count, scale)
    by_target[...] = spread(factors[:, 0:1], block)
    by_hidden[...] = spread(factors[:, 1:2], block)
    loss_ref[...] = jnp.broadcast_to(loss, loss_ref.shape)
    squares[...] = jnp.zeros_like(squares)
    inner[...] = jnp.zeros_like(inner)
    piece = width // blocks // 128 * 128
    keep = 1.0 - learn_rate * decay_rate

    def span(at):
        return pl.ds(pl.multiple_of(at * block, block), block)

    def update(at, current):
        cols = span(at)
        grad_rows = (
            c_ref[0, :, cols].astype(F32) * by_target[...] - h_ref[:, cols] * by_hidden[...]
        ).astype(BF16)
        for low in range(0, width, rows):
            part = pl.ds(low, rows)
            product = jnp.dot(xt_ref[part, :], grad_rows, preferred_element_type=F32)
            g_ref[part, cols] = product.astype(BF16)
            moved = product / (jnp.abs(product) + adam_eps / scale)
            current[part, :] = (
                keep * w_ref[part, cols].astype(F32) - learn_rate * moved
            ).astype(BF16)
        flip = pl.ds(pl.multiple_of(at * piece, 128), piece)
        xt2_ref[flip, :] = x_ref[1, :, flip].T

    def project(at, current):
        cols = span(at)
        hidden = jnp.dot(x_ref[1], current[...], preferred_element_type=F32)
        h2_ref[:, cols] = hidden
        squares[...] += lane_fold(hidden * hidden)
        inner[...] += lane_fold(c_ref[1, :, cols].astype(F32) * hidden)

    def pair(at, carry):
        update(2 * at + 1, odd)
        project(2 * at, even)
        update(2 * at + 2, even)
        project(2 * at + 1, odd)
        return carry

    update(0, even)
    lax.fori_loop(0, (blocks - 1) // 2, pair, 0)
    if blocks % 2:
        project(blocks - 1, even)
    else:
        update(blocks - 1, odd)
        project(blocks - 2, even)
        project(blocks - 1, odd)
    if piece * blocks < width:
        xt2_ref[piece * blocks :, :] = x_ref[1, :, piece * blocks :].T
    write_stats(stats_ref, squares, inner)


def middle(stats, flipped, tokens, weight, hidden, target, units):
    _, count, width = tokens.shape
    columns = weight.shape[1]
    block = width_block(columns)
    whole = pl.BlockSpec(memory_space=pltpu.VMEM)
    return pl.pallas_call(
        functools.partial(
            middle_kernel, scale=width**-0.5, units=units, rows=min(ROWS, width), block=block
        ),
        out_shape=(
            pltpu.VMEM((width, columns), BF16),
            pltpu.VMEM((count, columns), F32),
            pltpu.VMEM((width, count), BF16),
            jax.ShapeDtypeStruct((2, count), F32),
            jax.ShapeDtypeStruct((1, 128), F32),
        ),
        in_specs=[[whole] * len(stats)] + [whole] * 5,
        out_specs=(whole,) * 5,
        scratch_shapes=[
            pltpu.VMEM((count, block), F32),
            pltpu.VMEM((count, block), F32),
            pltpu.VMEM((width, block), BF16),
            pltpu.VMEM((width, block), BF16),
            pltpu.VMEM((count, 128), F32),
            pltpu.VMEM((count, 128), F32),
        ],
        compiler_params=pltpu.CompilerParams(vmem_limit_bytes=KERNEL_VMEM),
        name="middle",
    )(stats, flipped, tokens, weight, hidden, target)


def factors_kernel(*refs, units, scale):
    parts, (by_target, by_hidden, loss_ref) = refs[:-3], refs[-3:]
    count = by_target.shape[0]
    factors, loss = token_factors(tree_sum([part[...] for part in parts]), units, count, scale)
    by_target[...] = spread(factors[:, 0:1], LANES)
    by_hidden[...] = spread(factors[:, 1:2], LANES)
    loss_ref[...] = jnp.broadcast_to(loss, loss_ref.shape)


def last_part(
    by_target, by_hidden, xt_ref, w_ref, g_ref, h_ref, c_ref, final_ref, grad_rows,
    *, scale, tall, cols, rows,
):
    count = h_ref.shape[0]
    low, block = cols.start, cols.stop - cols.start

    def prepare(at, carry):
        part = pl.ds(pl.multiple_of(at * TOKEN_ROWS, TOKEN_ROWS), TOKEN_ROWS)
        for lane in range(0, block, LANES):
            here = slice(low + lane, low + lane + LANES)
            grad_rows[part, lane : lane + LANES] = (
                c_ref[1, part, here].astype(F32) * by_target[part, :]
                - h_ref[part, here] * by_hidden[part, :]
            ).astype(BF16)
        return carry

    lax.fori_loop(0, count // TOKEN_ROWS, prepare, 0)
    bias_first = 1.0 - beta_first**2
    bias_second = 1.0 - beta_second**2
    old_moment = learn_rate * scale * beta_first * (1.0 - beta_first) / bias_first
    new_moment = learn_rate * scale * (1.0 - beta_first) / bias_first
    old_second = scale * scale * beta_second * (1.0 - beta_second) / bias_second
    new_second = scale * scale * (1.0 - beta_second) / bias_second
    keep = 1.0 - learn_rate * decay_rate

    def one(at, carry):
        here = pl.ds(pl.multiple_of(at * rows, rows), rows)
        part = pl.ds(pl.multiple_of(tall.start + at * rows, rows), rows)
        product = jnp.dot(xt_ref[part, :], grad_rows[...], preferred_element_type=F32)
        first = g_ref[part, cols].astype(F32)
        moved = first / (jnp.abs(first) + adam_eps / scale)
        moment = old_moment * first + new_moment * product
        second = old_second * (first * first) + new_second * (product * product)
        second = jnp.maximum(second, tiny_square)
        fresh = moment / (second * lax.rsqrt(second) + adam_eps)
        master = keep * keep * w_ref[part, cols].astype(F32)
        final_ref[here, :] = (master - (keep * learn_rate * moved + fresh)).astype(BF16)
        return carry

    lax.fori_loop(0, final_ref.shape[0] // rows, one, 0)


def first_piece_kernel(*refs, units, parts, scale, **sizes):
    stats, operands, outs, grad_rows = refs[:parts], refs[parts:-5], refs[-5:-1], refs[-1]
    final_ref, by_target, by_hidden, loss_ref = outs
    factors_kernel(*stats, by_target, by_hidden, loss_ref, units=units, scale=scale)
    last_part(by_target, by_hidden, *operands, final_ref, grad_rows, scale=scale, **sizes)


def piece_call(kernel, outs, operands, tall, cols, count, units):
    whole = pl.BlockSpec(memory_space=pltpu.VMEM)
    height, block = tall.stop - tall.start, cols.stop - cols.start
    width = operands[-4].shape[0]
    return pl.pallas_call(
        functools.partial(
            kernel, scale=width**-0.5, tall=tall, cols=cols, rows=min(PIECE_CELLS // block, height), **units
        ),
        out_shape=(pltpu.VMEM((height, block), BF16), *outs),
        in_specs=[whole] * len(operands),
        out_specs=(whole,) * (1 + len(outs)),
        scratch_shapes=[pltpu.VMEM((count, block), BF16)],
        compiler_params=pltpu.CompilerParams(vmem_limit_bytes=KERNEL_VMEM),
        cost_estimate=pl.CostEstimate(
            flops=2 * height * count * block,
            bytes_accessed=2 * height * (3 * block + count) + 6 * count * block,
            transcendentals=3 * height * block,
        ),
    )(*operands)


def first_piece(stats, operands, units, tall, cols):
    count = operands[0].shape[1]
    outs = (
        pltpu.VMEM((count, LANES), F32),
        pltpu.VMEM((count, LANES), F32),
        jax.ShapeDtypeStruct((1, LANES), F32),
    )
    extra = {"units": units, "parts": len(stats)}
    return piece_call(first_piece_kernel, outs, (*stats, *operands), tall, cols, count, extra)


def next_piece(factors, operands, tall, cols):
    count = operands[0].shape[1]
    return piece_call(last_part, (), (*factors, *operands), tall, cols, count, {})[0]


def losses_kernel(first_ref, second_ref, out_ref, buffer, sem):
    buffer[:, 0:1] = first_ref[:, 0:1]
    buffer[:, 1:2] = second_ref[:, 0:1]
    copy = pltpu.make_async_copy(buffer, out_ref, sem)
    copy.start()
    copy.wait()


def losses_out(first, second):
    whole = pl.BlockSpec(memory_space=pltpu.VMEM)
    return pl.pallas_call(
        losses_kernel,
        out_shape=pltpu.HBM((1, 2), F32),
        in_specs=[whole, whole],
        out_specs=pl.BlockSpec(memory_space=pl.ANY),
        scratch_shapes=[pltpu.VMEM((1, 2), F32), pltpu.SemaphoreType.DMA(())],
        compiler_params=pltpu.CompilerParams(vmem_limit_bytes=KERNEL_VMEM),
        name="losses",
    )(first, second)


def mean_kernel(own_ref, peer_ref, *refs, tall, cols, parts):
    out_ref, buffer, sems = refs[-3:]
    height, block = own_ref.shape
    rows = height // parts
    step = min(MEAN_CELLS // block, rows)

    def copy(at):
        part = pl.ds(pl.multiple_of(at * rows, rows), rows)
        there = pl.ds(pl.multiple_of(tall.start + at * rows, rows), rows)
        return pltpu.make_async_copy(buffer.at[part, :], out_ref.at[there, cols], sems.at[at])

    def one(at, carry):
        def inner(sub, carry):
            part = pl.ds(pl.multiple_of(at * rows + sub * step, step), step)
            buffer[part, :] = (
                (own_ref[part, :].astype(F32) + peer_ref[part, :].astype(F32)) * 0.5
            ).astype(BF16)
            return carry

        lax.fori_loop(0, rows // step, inner, 0)
        copy(at).start()
        return carry

    lax.fori_loop(0, parts, one, 0)
    for at in range(parts):
        copy(at).wait()


def mean_into(out, own, peer, shape, tall, cols):
    height, block = own.shape
    parts = 4 if height % (4 * LANES) == 0 else 1
    whole = pl.BlockSpec(memory_space=pltpu.VMEM)
    anywhere = pl.BlockSpec(memory_space=pl.ANY)
    return pl.pallas_call(
        functools.partial(mean_kernel, tall=tall, cols=cols, parts=parts),
        out_shape=jax.ShapeDtypeStruct(shape, BF16),
        in_specs=[whole, whole] + ([] if out is None else [anywhere]),
        out_specs=anywhere,
        scratch_shapes=[
            pltpu.VMEM((height, block), BF16),
            pltpu.SemaphoreType.DMA((parts,)),
        ],
        input_output_aliases={} if out is None else {2: 0},
        compiler_params=pltpu.CompilerParams(vmem_limit_bytes=KERNEL_VMEM),
        cost_estimate=pl.CostEstimate(
            flops=2 * height * block, bytes_accessed=6 * height * block, transcendentals=0
        ),
        name="mean",
    )(*([own, peer] + ([] if out is None else [out])))


def tree_sum(parts):
    while len(parts) > 1:
        parts = [parts[at] + parts[at + 1] for at in range(0, len(parts), 2)]
    return parts[0]


def everyones(array, axis):
    devices = lax.axis_size(axis)
    if devices & (devices - 1):
        return [lax.psum(array, axis)]
    return [array] + [
        lax.ppermute(array, axis, [(i, i ^ flip) for i in range(devices)])
        for flip in range(1, devices)
    ]


def shifted(array, axis, by):
    devices = lax.axis_size(axis)
    return lax.ppermute(array, axis, [(i, (i + by) % devices) for i in range(devices)])


def shards(weight, tokens, cotangent, batch_order, step_index):
    weight, tokens, target, order = weight[0], tokens[0], cotangent[0], batch_order[0]
    width, columns = weight.shape
    units = columns * lax.axis_size("tp")
    levels = lax.axis_size("rep").bit_length() - 1
    hop_level = lax.rem(step_index[0], levels)

    pieces = chunks_of(width, columns)

    def chain(exponent):
        def run(order, tokens, weight, target):
            hidden, flipped, stats, tokens, weight, target = forward(order, tokens, weight, target)
            stats = everyones(stats, "tp")
            gradient, hidden, flipped, stats, loss_first = middle(
                stats, flipped, tokens, weight, hidden, target, units
            )
            stats = everyones(stats, "tp")
            finals, peers = [], []
            operands = (flipped, weight, gradient, hidden, target)
            for at, piece in enumerate(pieces):
                if at == 0:
                    final, *factors, loss_second = first_piece(stats, operands, units, *piece)
                else:
                    final = next_piece(factors, operands, *piece)
                finals.append(final)
                peers.append(shifted(final, "rep", 2**exponent))
            out = None
            for piece, final, peer in zip(pieces, finals, peers):
                out = mean_into(out, final, peer, weight.shape, *piece)
            return out, losses_out(loss_first, loss_second)

        return run

    averaged, losses = lax.switch(
        hop_level, [chain(exponent) for exponent in range(levels)], order, tokens, weight, target
    )
    return (averaged[None], losses)


def solution(mesh):
    placed = (
        P("rep", None, "tp"),
        P("rep", None, None, None),
        P("rep", None, None, "tp"),
        P("rep", None),
        P(),
    )
    return jax.shard_map(
        shards,
        mesh=mesh,
        in_specs=placed,
        out_specs=(P("rep", None, "tp"), P("rep", None)),
        check_vma=False,
    )
```

```python
import functools

import jax
import jax.numpy as jnp
from jax import lax
from jax.experimental import pallas as pl
from jax.experimental.pallas import tpu as pltpu
from jax.sharding import PartitionSpec as P


beta_first = 0.9
beta_second = 0.95
learn_rate = 0.05
decay_rate = 0.1
adam_eps = 1e-05
norm_eps = 1e-06
tiny_square = 1e-30

F32 = jnp.float32
BF16 = jnp.bfloat16
KERNEL_VMEM = 16 * 1024 * 1024
ROWS = 256
LANES = 128
TOKEN_ROWS = 64
FIRST_CELLS = 256 * 256
PIECE_CELLS = 128 * 256
MEAN_CELLS = 128 * 256
PIECE_COLUMNS = 512
AHEAD = 3


def width_block(columns):
    for block in (256, 128):
        if columns % block == 0:
            return block
    return columns


def chunks_of(width, columns):
    if columns % LANES or columns <= 2 * LANES or width % (4 * LANES):
        return [(slice(0, width), slice(0, columns))]
    halves = (slice(0, width // 2), slice(width // 2, width))
    pieces = [(half, slice(0, LANES)) for half in halves]
    low = LANES
    while low < columns - LANES:
        high = min(low + PIECE_COLUMNS, columns - LANES)
        pieces.append((slice(0, width), slice(low, high)))
        low = high
    return pieces + [(half, slice(low, columns)) for half in halves]


def lane_fold(values):
    total = values[:, :128]
    for at in range(128, values.shape[1], 128):
        total = total + values[:, at : at + 128]
    return total


def write_stats(stats_ref, squares, inner):
    stats_ref[0:1, :] = jnp.sum(squares[...].T, axis=0, keepdims=True)
    stats_ref[1:2, :] = jnp.sum(inner[...].T, axis=0, keepdims=True)


def token_factors(stats, units, tokens, scale):
    squares, inner = stats[0:1, :] * (scale * scale), stats[1:2, :] * scale
    radius = jnp.sqrt(squares / units + norm_eps)
    loss = jnp.sum(inner / radius, axis=1, keepdims=True) / tokens
    by_target = 1.0 / (radius * tokens)
    by_hidden = scale * inner / (units * radius * radius * radius * tokens)
    pad = jnp.zeros((6, stats.shape[1]), F32)
    columns = jnp.concatenate([by_target, by_hidden, pad], axis=0).T
    return columns, loss


def spread(column, lanes):
    return jnp.broadcast_to(column, (column.shape[0], lanes))


def in_hbm(array):
    return pltpu.with_memory_space_constraint(array, pltpu.HBM)


def forward_kernel(
    order_hbm, x_hbm, w_hbm, c_hbm, h_ref, xt_ref, stats_ref, x_ref, w_ref, c_ref,
    order, squares, inner, order_sem, x_sem, w_sem, c_sem, *, block,
):
    width, columns = w_ref.shape
    blocks = columns // block
    order_copy = pltpu.make_async_copy(order_hbm, order, order_sem)
    order_copy.start()

    def w_copy(at):
        part = pl.ds(pl.multiple_of(at * block, block), block)
        return pltpu.make_async_copy(w_hbm.at[:, part], w_ref.at[:, part], w_sem.at[at])

    w_copy(0).start()
    squares[...] = jnp.zeros_like(squares)
    inner[...] = jnp.zeros_like(inner)
    piece = width // blocks // 128 * 128
    order_copy.wait()
    first, second = order[0], order[1]

    def x_copy(at, chosen):
        return pltpu.make_async_copy(x_hbm.at[chosen], x_ref.at[at], x_sem.at[at])

    def c_copy(at):
        part = pl.ds(pl.multiple_of(at * block, block), block)
        return pltpu.make_async_copy(c_hbm.at[first, :, part], c_ref.at[0, :, part], c_sem.at[at])

    later = pltpu.make_async_copy(c_hbm.at[second], c_ref.at[1], c_sem.at[blocks])
    x_copy(0, first).start()
    c_copy(0).start()
    for at in range(1, min(AHEAD, blocks)):
        w_copy(at).start(priority=1)
        c_copy(at).start(priority=1)
    x_copy(0, first).wait()

    def one(at, carry):
        @pl.when(at + AHEAD < blocks)
        def _():
            w_copy(at + AHEAD).start(priority=1)
            c_copy(at + AHEAD).start(priority=1)

        @pl.when(at + AHEAD == blocks)
        def _():
            x_copy(1, second).start(priority=1)
            later.start(priority=1)

        w_copy(at).wait()
        c_copy(at).wait()
        part = pl.ds(pl.multiple_of(at * block, block), block)
        hidden = jnp.dot(x_ref[0], w_ref[:, part], preferred_element_type=F32)
        h_ref[:, part] = hidden
        target = c_ref[0, :, part].astype(F32)
        squares[...] += lane_fold(hidden * hidden)
        inner[...] += lane_fold(target * hidden)
        flip = pl.ds(pl.multiple_of(at * piece, 128), piece)
        xt_ref[flip, :] = x_ref[0, :, flip].T
        return carry

    lax.fori_loop(0, blocks, one, 0)
    if blocks < AHEAD:
        x_copy(1, second).start()
        later.start()
    if piece * blocks < width:
        xt_ref[piece * blocks :, :] = x_ref[0, :, piece * blocks :].T
    write_stats(stats_ref, squares, inner)
    x_copy(1, second).wait()
    later.wait()


def forward(order, tokens, weight, target):
    steps, count, width = tokens.shape
    columns = weight.shape[1]
    block = width_block(columns)
    blocks = columns // block
    whole = pl.BlockSpec(memory_space=pltpu.VMEM)
    return pl.pallas_call(
        functools.partial(forward_kernel, block=block),
        out_shape=(
            pltpu.VMEM((count, columns), F32),
            pltpu.VMEM((width, count), BF16),
            jax.ShapeDtypeStruct((2, count), F32),
            pltpu.VMEM(tokens.shape, BF16),
            pltpu.VMEM(weight.shape, BF16),
            pltpu.VMEM(target.shape, BF16),
        ),
        in_specs=[pl.BlockSpec(memory_space=pl.ANY)] * 4,
        out_specs=(whole,) * 6,
        scratch_shapes=[
            pltpu.SMEM(order.shape, order.dtype),
            pltpu.VMEM((count, 128), F32),
            pltpu.VMEM((count, 128), F32),
            pltpu.SemaphoreType.DMA(()),
            pltpu.SemaphoreType.DMA((steps,)),
            pltpu.SemaphoreType.DMA((blocks,)),
            pltpu.SemaphoreType.DMA((blocks + 1,)),
        ],
        compiler_params=pltpu.CompilerParams(vmem_limit_bytes=KERNEL_VMEM),
        name="forward_first",
    )(in_hbm(order), in_hbm(tokens), in_hbm(weight), in_hbm(target))


def middle_kernel(
    parts, xt_ref, x_ref, w_ref, h_ref, c_ref,
    g_ref, h2_ref, xt2_ref, stats_ref, loss_ref,
    by_target, by_hidden, even, odd, squares, inner, *, scale, units, rows, block,
):
    count, columns = h_ref.shape
    width = w_ref.shape[0]
    blocks = columns // block
    factors, loss = token_factors(tree_sum([part[...] for part in parts]), units, count, scale)
    by_target[...] = spread(factors[:, 0:1], block)
    by_hidden[...] = spread(factors[:, 1:2], block)
    loss_ref[...] = jnp.broadcast_to(loss, loss_ref.shape)
    squares[...] = jnp.zeros_like(squares)
    inner[...] = jnp.zeros_like(inner)
    piece = width // blocks // 128 * 128
    keep = 1.0 - learn_rate * decay_rate

    def span(at):
        return pl.ds(pl.multiple_of(at * block, block), block)

    def update(at, current):
        cols = span(at)
        grad_rows = (
            c_ref[0, :, cols].astype(F32) * by_target[...] - h_ref[:, cols] * by_hidden[...]
        ).astype(BF16)
        for low in range(0, width, rows):
            part = pl.ds(low, rows)
            product = jnp.dot(xt_ref[part, :], grad_rows, preferred_element_type=F32)
            g_ref[part, cols] = product.astype(BF16)
            moved = product / (jnp.abs(product) + adam_eps / scale)
            current[part, :] = (
                keep * w_ref[part, cols].astype(F32) - learn_rate * moved
            ).astype(BF16)
        flip = pl.ds(pl.multiple_of(at * piece, 128), piece)
        xt2_ref[flip, :] = x_ref[1, :, flip].T

    def project(at, current):
        cols = span(at)
        hidden = jnp.dot(x_ref[1], current[...], preferred_element_type=F32)
        h2_ref[:, cols] = hidden
        squares[...] += lane_fold(hidden * hidden)
        inner[...] += lane_fold(c_ref[1, :, cols].astype(F32) * hidden)

    def pair(at, carry):
        update(2 * at + 1, odd)
        project(2 * at, even)
        update(2 * at + 2, even)
        project(2 * at + 1, odd)
        return carry

    update(0, even)
    lax.fori_loop(0, (blocks - 1) // 2, pair, 0)
    if blocks % 2:
        project(blocks - 1, even)
    else:
        update(blocks - 1, odd)
        project(blocks - 2, even)
        project(blocks - 1, odd)
    if piece * blocks < width:
        xt2_ref[piece * blocks :, :] = x_ref[1, :, piece * blocks :].T
    write_stats(stats_ref, squares, inner)


def middle(stats, flipped, tokens, weight, hidden, target, units):
    _, count, width = tokens.shape
    columns = weight.shape[1]
    block = width_block(columns)
    whole = pl.BlockSpec(memory_space=pltpu.VMEM)
    return pl.pallas_call(
        functools.partial(
            middle_kernel, scale=width**-0.5, units=units, rows=min(ROWS, width), block=block
        ),
        out_shape=(
            pltpu.VMEM((width, columns), BF16),
            pltpu.VMEM((count, columns), F32),
            pltpu.VMEM((width, count), BF16),
            jax.ShapeDtypeStruct((2, count), F32),
            jax.ShapeDtypeStruct((1, 128), F32),
        ),
        in_specs=[[whole] * len(stats)] + [whole] * 5,
        out_specs=(whole,) * 5,
        scratch_shapes=[
            pltpu.VMEM((count, block), F32),
            pltpu.VMEM((count, block), F32),
            pltpu.VMEM((width, block), BF16),
            pltpu.VMEM((width, block), BF16),
            pltpu.VMEM((count, 128), F32),
            pltpu.VMEM((count, 128), F32),
        ],
        compiler_params=pltpu.CompilerParams(vmem_limit_bytes=KERNEL_VMEM),
        name="middle",
    )(stats, flipped, tokens, weight, hidden, target)


def factors_kernel(*refs, units, scale):
    parts, (by_target, by_hidden, loss_ref) = refs[:-3], refs[-3:]
    count = by_target.shape[0]
    factors, loss = token_factors(tree_sum([part[...] for part in parts]), units, count, scale)
    by_target[...] = spread(factors[:, 0:1], LANES)
    by_hidden[...] = spread(factors[:, 1:2], LANES)
    loss_ref[...] = jnp.broadcast_to(loss, loss_ref.shape)


def last_part(
    by_target, by_hidden, xt_ref, w_ref, g_ref, h_ref, c_ref, final_ref, grad_rows,
    *, scale, tall, cols, rows,
):
    count = h_ref.shape[0]
    low, block = cols.start, cols.stop - cols.start

    def prepare(at, carry):
        part = pl.ds(pl.multiple_of(at * TOKEN_ROWS, TOKEN_ROWS), TOKEN_ROWS)
        for lane in range(0, block, LANES):
            here = slice(low + lane, low + lane + LANES)
            grad_rows[part, lane : lane + LANES] = (
                c_ref[1, part, here].astype(F32) * by_target[part, :]
                - h_ref[part, here] * by_hidden[part, :]
            ).astype(BF16)
        return carry

    lax.fori_loop(0, count // TOKEN_ROWS, prepare, 0)
    bias_first = 1.0 - beta_first**2
    bias_second = 1.0 - beta_second**2
    old_moment = learn_rate * scale * beta_first * (1.0 - beta_first) / bias_first
    new_moment = learn_rate * scale * (1.0 - beta_first) / bias_first
    old_second = scale * scale * beta_second * (1.0 - beta_second) / bias_second
    new_second = scale * scale * (1.0 - beta_second) / bias_second
    keep = 1.0 - learn_rate * decay_rate

    def one(at, carry):
        here = pl.ds(pl.multiple_of(at * rows, rows), rows)
        part = pl.ds(pl.multiple_of(tall.start + at * rows, rows), rows)
        product = jnp.dot(xt_ref[part, :], grad_rows[...], preferred_element_type=F32)
        first = g_ref[part, cols].astype(F32)
        moved = first / (jnp.abs(first) + adam_eps / scale)
        moment = old_moment * first + new_moment * product
        second = old_second * (first * first) + new_second * (product * product)
        second = jnp.maximum(second, tiny_square)
        fresh = moment / (second * lax.rsqrt(second) + adam_eps)
        master = keep * keep * w_ref[part, cols].astype(F32)
        final_ref[here, :] = (master - (keep * learn_rate * moved + fresh)).astype(BF16)
        return carry

    lax.fori_loop(0, final_ref.shape[0] // rows, one, 0)


def first_piece_kernel(*refs, units, parts, scale, **sizes):
    stats, operands, outs, grad_rows = refs[:parts], refs[parts:-5], refs[-5:-1], refs[-1]
    final_ref, by_target, by_hidden, loss_ref = outs
    factors_kernel(*stats, by_target, by_hidden, loss_ref, units=units, scale=scale)
    last_part(by_target, by_hidden, *operands, final_ref, grad_rows, scale=scale, **sizes)


def piece_call(kernel, name, outs, operands, tall, cols, count, units):
    whole = pl.BlockSpec(memory_space=pltpu.VMEM)
    height, block = tall.stop - tall.start, cols.stop - cols.start
    width = operands[-4].shape[0]
    cells = PIECE_CELLS if name == "next_piece" else FIRST_CELLS
    return pl.pallas_call(
        functools.partial(
            kernel, scale=width**-0.5, tall=tall, cols=cols, rows=min(cells // block, height), **units
        ),
        out_shape=(pltpu.VMEM((height, block), BF16), *outs),
        in_specs=[whole] * len(operands),
        out_specs=(whole,) * (1 + len(outs)),
        scratch_shapes=[pltpu.VMEM((count, block), BF16)],
        compiler_params=pltpu.CompilerParams(vmem_limit_bytes=KERNEL_VMEM),
        cost_estimate=pl.CostEstimate(
            flops=2 * height * count * block,
            bytes_accessed=2 * height * (3 * block + count) + 6 * count * block,
            transcendentals=3 * height * block,
        ),
    )(*operands)


def first_piece(stats, operands, units, tall, cols):
    count = operands[0].shape[1]
    outs = (
        pltpu.VMEM((count, LANES), F32),
        pltpu.VMEM((count, LANES), F32),
        jax.ShapeDtypeStruct((1, LANES), F32),
    )
    extra = {"units": units, "parts": len(stats)}
    return piece_call(
        first_piece_kernel, "first_piece", outs, (*stats, *operands), tall, cols, count, extra
    )


def next_piece(factors, operands, tall, cols):
    count = operands[0].shape[1]
    return piece_call(last_part, "next_piece", (), (*factors, *operands), tall, cols, count, {})[0]


def losses_kernel(first_ref, second_ref, out_ref, buffer, sem):
    buffer[:, 0:1] = first_ref[:, 0:1]
    buffer[:, 1:2] = second_ref[:, 0:1]
    copy = pltpu.make_async_copy(buffer, out_ref, sem)
    copy.start()
    copy.wait()


def losses_out(first, second):
    whole = pl.BlockSpec(memory_space=pltpu.VMEM)
    return pl.pallas_call(
        losses_kernel,
        out_shape=pltpu.HBM((1, 2), F32),
        in_specs=[whole, whole],
        out_specs=pl.BlockSpec(memory_space=pl.ANY),
        scratch_shapes=[pltpu.VMEM((1, 2), F32), pltpu.SemaphoreType.DMA(())],
        compiler_params=pltpu.CompilerParams(vmem_limit_bytes=KERNEL_VMEM),
        name="losses",
    )(first, second)


def mean_kernel(own_ref, peer_ref, *refs, tall, cols, parts):
    out_ref, buffer, sems = refs[-3:]
    height, block = own_ref.shape
    rows = height // parts
    step = min(MEAN_CELLS // block, rows)

    def copy(at):
        part = pl.ds(pl.multiple_of(at * rows, rows), rows)
        there = pl.ds(pl.multiple_of(tall.start + at * rows, rows), rows)
        return pltpu.make_async_copy(buffer.at[part, :], out_ref.at[there, cols], sems.at[at])

    def one(at, carry):
        def inner(sub, carry):
            part = pl.ds(pl.multiple_of(at * rows + sub * step, step), step)
            buffer[part, :] = (
                (own_ref[part, :].astype(F32) + peer_ref[part, :].astype(F32)) * 0.5
            ).astype(BF16)
            return carry

        lax.fori_loop(0, rows // step, inner, 0)
        copy(at).start()
        return carry

    lax.fori_loop(0, parts, one, 0)
    for at in range(parts):
        copy(at).wait()


def mean_into(out, own, peer, shape, tall, cols):
    height, block = own.shape
    parts = 4 if height % (4 * LANES) == 0 else 1
    whole = pl.BlockSpec(memory_space=pltpu.VMEM)
    anywhere = pl.BlockSpec(memory_space=pl.ANY)
    return pl.pallas_call(
        functools.partial(mean_kernel, tall=tall, cols=cols, parts=parts),
        out_shape=jax.ShapeDtypeStruct(shape, BF16),
        in_specs=[whole, whole] + ([] if out is None else [anywhere]),
        out_specs=anywhere,
        scratch_shapes=[
            pltpu.VMEM((height, block), BF16),
            pltpu.SemaphoreType.DMA((parts,)),
        ],
        input_output_aliases={} if out is None else {2: 0},
        compiler_params=pltpu.CompilerParams(vmem_limit_bytes=KERNEL_VMEM),
        cost_estimate=pl.CostEstimate(
            flops=2 * height * block, bytes_accessed=6 * height * block, transcendentals=0
        ),
        name="mean",
    )(*([own, peer] + ([] if out is None else [out])))


def tree_sum(parts):
    while len(parts) > 1:
        parts = [parts[at] + parts[at + 1] for at in range(0, len(parts), 2)]
    return parts[0]


def everyones(array, axis):
    devices = lax.axis_size(axis)
    if devices & (devices - 1):
        return [lax.psum(array, axis)]
    return [array] + [
        lax.ppermute(array, axis, [(i, i ^ flip) for i in range(devices)])
        for flip in range(1, devices)
    ]


def shifted(array, axis, by):
    devices = lax.axis_size(axis)
    return lax.ppermute(array, axis, [(i, (i + by) % devices) for i in range(devices)])


def shards(weight, tokens, cotangent, batch_order, step_index):
    weight, tokens, target, order = weight[0], tokens[0], cotangent[0], batch_order[0]
    width, columns = weight.shape
    units = columns * lax.axis_size("tp")
    levels = lax.axis_size("rep").bit_length() - 1
    hop_level = lax.rem(step_index[0], levels)

    pieces = chunks_of(width, columns)

    def chain(exponent):
        def run(order, tokens, weight, target):
            hidden, flipped, stats, tokens, weight, target = forward(order, tokens, weight, target)
            stats = everyones(stats, "tp")
            gradient, hidden, flipped, stats, loss_first = middle(
                stats, flipped, tokens, weight, hidden, target, units
            )
            stats = everyones(stats, "tp")
            finals, peers = [], []
            operands = (flipped, weight, gradient, hidden, target)
            for at, piece in enumerate(pieces):
                if at == 0:
                    final, *factors, loss_second = first_piece(stats, operands, units, *piece)
                else:
                    final = next_piece(factors, operands, *piece)
                finals.append(final)
                peers.append(shifted(final, "rep", 2**exponent))
            out = None
            for piece, final, peer in zip(pieces, finals, peers):
                out = mean_into(out, final, peer, weight.shape, *piece)
            return out, losses_out(loss_first, loss_second)

        return run

    averaged, losses = lax.switch(
        hop_level, [chain(exponent) for exponent in range(levels)], order, tokens, weight, target
    )
    return (averaged[None], losses)


def solution(mesh):
    placed = (
        P("rep", None, "tp"),
        P("rep", None, None, None),
        P("rep", None, None, "tp"),
        P("rep", None),
        P(),
    )
    return jax.shard_map(
        shards,
        mesh=mesh,
        in_specs=placed,
        out_specs=(P("rep", None, "tp"), P("rep", None)),
        check_vma=False,
    )
```

```python
import functools

import jax
import jax.numpy as jnp
from jax import lax
from jax.experimental import pallas as pl
from jax.experimental.pallas import tpu as pltpu
from jax.sharding import PartitionSpec as P


beta_first = 0.9
beta_second = 0.95
learn_rate = 0.05
decay_rate = 0.1
adam_eps = 1e-05
norm_eps = 1e-06
tiny_square = 1e-30

F32 = jnp.float32
BF16 = jnp.bfloat16
KERNEL_VMEM = 16 * 1024 * 1024
ROWS = 256
LANES = 128
TOKEN_ROWS = 64
PIECE_COLUMNS = 384
AHEAD = 3


def width_block(columns):
    for block in (256, 128):
        if columns % block == 0:
            return block
    return columns


def chunks_of(width, columns):
    if columns % LANES or columns <= 2 * LANES or width % (4 * LANES):
        return [(slice(0, width), slice(0, columns))]
    halves = (slice(0, width // 2), slice(width // 2, width))
    pieces = [(half, slice(0, LANES)) for half in halves]
    low = LANES
    while low < columns - LANES:
        high = min(low + PIECE_COLUMNS, columns - LANES)
        pieces.append((slice(0, width), slice(low, high)))
        low = high
    return pieces + [(half, slice(low, columns)) for half in halves]


def lane_fold(values):
    total = values[:, :128]
    for at in range(128, values.shape[1], 128):
        total = total + values[:, at : at + 128]
    return total


def write_stats(stats_ref, squares, inner):
    stats_ref[0:1, :] = jnp.sum(squares[...].T, axis=0, keepdims=True)
    stats_ref[1:2, :] = jnp.sum(inner[...].T, axis=0, keepdims=True)


def token_factors(stats, units, tokens, scale):
    squares, inner = stats[0:1, :] * (scale * scale), stats[1:2, :] * scale
    radius = jnp.sqrt(squares / units + norm_eps)
    loss = jnp.sum(inner / radius, axis=1, keepdims=True) / tokens
    by_target = 1.0 / (radius * tokens)
    by_hidden = scale * inner / (units * radius * radius * radius * tokens)
    pad = jnp.zeros((6, stats.shape[1]), F32)
    columns = jnp.concatenate([by_target, by_hidden, pad], axis=0).T
    return columns, loss


def spread(column, lanes):
    return jnp.broadcast_to(column, (column.shape[0], lanes))


def in_hbm(array):
    return pltpu.with_memory_space_constraint(array, pltpu.HBM)


def forward_kernel(
    order_hbm, x_hbm, w_hbm, c_hbm, h_ref, xt_ref, stats_ref, x_ref, w_ref, c_ref,
    order, squares, inner, order_sem, x_sem, w_sem, c_sem, *, block,
):
    width, columns = w_ref.shape
    blocks = columns // block
    order_copy = pltpu.make_async_copy(order_hbm, order, order_sem)
    order_copy.start()

    def w_copy(at):
        part = pl.ds(pl.multiple_of(at * block, block), block)
        return pltpu.make_async_copy(w_hbm.at[:, part], w_ref.at[:, part], w_sem.at[at])

    w_copy(0).start()
    squares[...] = jnp.zeros_like(squares)
    inner[...] = jnp.zeros_like(inner)
    piece = width // blocks // 128 * 128
    order_copy.wait()
    first, second = order[0], order[1]

    def x_copy(at, chosen):
        return pltpu.make_async_copy(x_hbm.at[chosen], x_ref.at[at], x_sem.at[at])

    def c_copy(at):
        part = pl.ds(pl.multiple_of(at * block, block), block)
        return pltpu.make_async_copy(c_hbm.at[first, :, part], c_ref.at[0, :, part], c_sem.at[at])

    later = pltpu.make_async_copy(c_hbm.at[second], c_ref.at[1], c_sem.at[blocks])
    x_copy(0, first).start()
    c_copy(0).start()
    for at in range(1, min(AHEAD, blocks)):
        w_copy(at).start(priority=1)
        c_copy(at).start(priority=1)
    x_copy(0, first).wait()

    def one(at, carry):
        @pl.when(at + AHEAD < blocks)
        def _():
            w_copy(at + AHEAD).start(priority=1)
            c_copy(at + AHEAD).start(priority=1)

        @pl.when(at + AHEAD == blocks)
        def _():
            x_copy(1, second).start(priority=1)
            later.start(priority=1)

        w_copy(at).wait()
        c_copy(at).wait()
        part = pl.ds(pl.multiple_of(at * block, block), block)
        hidden = jnp.dot(x_ref[0], w_ref[:, part], preferred_element_type=F32)
        h_ref[:, part] = hidden
        target = c_ref[0, :, part].astype(F32)
        squares[...] += lane_fold(hidden * hidden)
        inner[...] += lane_fold(target * hidden)
        flip = pl.ds(pl.multiple_of(at * piece, 128), piece)
        xt_ref[flip, :] = x_ref[0, :, flip].T
        return carry

    lax.fori_loop(0, blocks, one, 0)
    if blocks < AHEAD:
        x_copy(1, second).start()
        later.start()
    if piece * blocks < width:
        xt_ref[piece * blocks :, :] = x_ref[0, :, piece * blocks :].T
    write_stats(stats_ref, squares, inner)
    x_copy(1, second).wait()
    later.wait()


def forward(order, tokens, weight, target):
    steps, count, width = tokens.shape
    columns = weight.shape[1]
    block = width_block(columns)
    blocks = columns // block
    whole = pl.BlockSpec(memory_space=pltpu.VMEM)
    return pl.pallas_call(
        functools.partial(forward_kernel, block=block),
        out_shape=(
            pltpu.VMEM((count, columns), F32),
            pltpu.VMEM((width, count), BF16),
            jax.ShapeDtypeStruct((2, count), F32),
            pltpu.VMEM(tokens.shape, BF16),
            pltpu.VMEM(weight.shape, BF16),
            pltpu.VMEM(target.shape, BF16),
        ),
        in_specs=[pl.BlockSpec(memory_space=pl.ANY)] * 4,
        out_specs=(whole,) * 6,
        scratch_shapes=[
            pltpu.SMEM(order.shape, order.dtype),
            pltpu.VMEM((count, 128), F32),
            pltpu.VMEM((count, 128), F32),
            pltpu.SemaphoreType.DMA(()),
            pltpu.SemaphoreType.DMA((steps,)),
            pltpu.SemaphoreType.DMA((blocks,)),
            pltpu.SemaphoreType.DMA((blocks + 1,)),
        ],
        compiler_params=pltpu.CompilerParams(vmem_limit_bytes=KERNEL_VMEM),
        name="forward_first",
    )(in_hbm(order), in_hbm(tokens), in_hbm(weight), in_hbm(target))


def middle_kernel(
    parts, xt_ref, x_ref, w_ref, h_ref, c_ref,
    g_ref, h2_ref, xt2_ref, stats_ref, loss_ref,
    by_target, by_hidden, even, odd, squares, inner, *, scale, units, rows, block,
):
    count, columns = h_ref.shape
    width = w_ref.shape[0]
    blocks = columns // block
    factors, loss = token_factors(tree_sum([part[...] for part in parts]), units, count, scale)
    by_target[...] = spread(factors[:, 0:1], block)
    by_hidden[...] = spread(factors[:, 1:2], block)
    loss_ref[...] = jnp.broadcast_to(loss, loss_ref.shape)
    squares[...] = jnp.zeros_like(squares)
    inner[...] = jnp.zeros_like(inner)
    piece = width // blocks // 128 * 128
    keep = 1.0 - learn_rate * decay_rate

    def span(at):
        return pl.ds(pl.multiple_of(at * block, block), block)

    def update(at, current):
        cols = span(at)
        grad_rows = (
            c_ref[0, :, cols].astype(F32) * by_target[...] - h_ref[:, cols] * by_hidden[...]
        ).astype(BF16)
        for low in range(0, width, rows):
            part = pl.ds(low, rows)
            product = jnp.dot(xt_ref[part, :], grad_rows, preferred_element_type=F32)
            g_ref[part, cols] = product.astype(BF16)
            moved = product / (jnp.abs(product) + adam_eps / scale)
            current[part, :] = (
                keep * w_ref[part, cols].astype(F32) - learn_rate * moved
            ).astype(BF16)
        flip = pl.ds(pl.multiple_of(at * piece, 128), piece)
        xt2_ref[flip, :] = x_ref[1, :, flip].T

    def project(at, current):
        cols = span(at)
        hidden = jnp.dot(x_ref[1], current[...], preferred_element_type=F32)
        h2_ref[:, cols] = hidden
        squares[...] += lane_fold(hidden * hidden)
        inner[...] += lane_fold(c_ref[1, :, cols].astype(F32) * hidden)

    def pair(at, carry):
        update(2 * at + 1, odd)
        project(2 * at, even)
        update(2 * at + 2, even)
        project(2 * at + 1, odd)
        return carry

    update(0, even)
    lax.fori_loop(0, (blocks - 1) // 2, pair, 0)
    if blocks % 2:
        project(blocks - 1, even)
    else:
        update(blocks - 1, odd)
        project(blocks - 2, even)
        project(blocks - 1, odd)
    if piece * blocks < width:
        xt2_ref[piece * blocks :, :] = x_ref[1, :, piece * blocks :].T
    write_stats(stats_ref, squares, inner)


def middle(stats, flipped, tokens, weight, hidden, target, units):
    _, count, width = tokens.shape
    columns = weight.shape[1]
    block = width_block(columns)
    whole = pl.BlockSpec(memory_space=pltpu.VMEM)
    return pl.pallas_call(
        functools.partial(
            middle_kernel, scale=width**-0.5, units=units, rows=min(ROWS, width), block=block
        ),
        out_shape=(
            pltpu.VMEM((width, columns), BF16),
            pltpu.VMEM((count, columns), F32),
            pltpu.VMEM((width, count), BF16),
            jax.ShapeDtypeStruct((2, count), F32),
            jax.ShapeDtypeStruct((1, 128), F32),
        ),
        in_specs=[[whole] * len(stats)] + [whole] * 5,
        out_specs=(whole,) * 5,
        scratch_shapes=[
            pltpu.VMEM((count, block), F32),
            pltpu.VMEM((count, block), F32),
            pltpu.VMEM((width, block), BF16),
            pltpu.VMEM((width, block), BF16),
            pltpu.VMEM((count, 128), F32),
            pltpu.VMEM((count, 128), F32),
        ],
        compiler_params=pltpu.CompilerParams(vmem_limit_bytes=KERNEL_VMEM),
        name="middle",
    )(stats, flipped, tokens, weight, hidden, target)


def factors_kernel(*refs, units, scale):
    parts, (by_target, by_hidden, loss_ref) = refs[:-3], refs[-3:]
    count = by_target.shape[0]
    factors, loss = token_factors(tree_sum([part[...] for part in parts]), units, count, scale)
    by_target[...] = spread(factors[:, 0:1], LANES)
    by_hidden[...] = spread(factors[:, 1:2], LANES)
    loss_ref[...] = jnp.broadcast_to(loss, loss_ref.shape)


def last_part(
    by_target, by_hidden, xt_ref, w_ref, g_ref, h_ref, c_ref, final_ref, grad_rows,
    *, scale, tall, cols, rows,
):
    count = h_ref.shape[0]
    low, block = cols.start, cols.stop - cols.start

    def prepare(at, carry):
        part = pl.ds(pl.multiple_of(at * TOKEN_ROWS, TOKEN_ROWS), TOKEN_ROWS)
        for lane in range(0, block, LANES):
            here = slice(low + lane, low + lane + LANES)
            grad_rows[part, lane : lane + LANES] = (
                c_ref[1, part, here].astype(F32) * by_target[part, :]
                - h_ref[part, here] * by_hidden[part, :]
            ).astype(BF16)
        return carry

    lax.fori_loop(0, count // TOKEN_ROWS, prepare, 0)
    bias_first = 1.0 - beta_first**2
    bias_second = 1.0 - beta_second**2
    old_moment = learn_rate * scale * beta_first * (1.0 - beta_first) / bias_first
    new_moment = learn_rate * scale * (1.0 - beta_first) / bias_first
    old_second = scale * scale * beta_second * (1.0 - beta_second) / bias_second
    new_second = scale * scale * (1.0 - beta_second) / bias_second
    keep = 1.0 - learn_rate * decay_rate

    def one(at, carry):
        here = pl.ds(pl.multiple_of(at * rows, rows), rows)
        part = pl.ds(pl.multiple_of(tall.start + at * rows, rows), rows)
        product = jnp.dot(xt_ref[part, :], grad_rows[...], preferred_element_type=F32)
        first = g_ref[part, cols].astype(F32)
        moved = first / (jnp.abs(first) + adam_eps / scale)
        moment = old_moment * first + new_moment * product
        second = old_second * (first * first) + new_second * (product * product)
        second = jnp.maximum(second, tiny_square)
        fresh = moment / (second * lax.rsqrt(second) + adam_eps)
        master = keep * keep * w_ref[part, cols].astype(F32)
        final_ref[here, :] = (master - (keep * learn_rate * moved + fresh)).astype(BF16)
        return carry

    lax.fori_loop(0, final_ref.shape[0] // rows, one, 0)


def first_piece_kernel(*refs, units, parts, scale, **sizes):
    stats, operands, outs, grad_rows = refs[:parts], refs[parts:-5], refs[-5:-1], refs[-1]
    final_ref, by_target, by_hidden, loss_ref = outs
    factors_kernel(*stats, by_target, by_hidden, loss_ref, units=units, scale=scale)
    last_part(by_target, by_hidden, *operands, final_ref, grad_rows, scale=scale, **sizes)


def piece_call(kernel, outs, operands, tall, cols, count, units):
    whole = pl.BlockSpec(memory_space=pltpu.VMEM)
    height, block = tall.stop - tall.start, cols.stop - cols.start
    width = operands[-4].shape[0]
    return pl.pallas_call(
        functools.partial(
            kernel, scale=width**-0.5, tall=tall, cols=cols, rows=min(512 if block <= LANES else 128, height), **units
        ),
        out_shape=(pltpu.VMEM((height, block), BF16), *outs),
        in_specs=[whole] * len(operands),
        out_specs=(whole,) * (1 + len(outs)),
        scratch_shapes=[pltpu.VMEM((count, block), BF16)],
        compiler_params=pltpu.CompilerParams(vmem_limit_bytes=KERNEL_VMEM),
        cost_estimate=pl.CostEstimate(
            flops=2 * height * count * block,
            bytes_accessed=2 * height * (3 * block + count) + 6 * count * block,
            transcendentals=3 * height * block,
        ),
    )(*operands)


def first_piece(stats, operands, units, tall, cols):
    count = operands[0].shape[1]
    outs = (
        pltpu.VMEM((count, LANES), F32),
        pltpu.VMEM((count, LANES), F32),
        jax.ShapeDtypeStruct((1, LANES), F32),
    )
    extra = {"units": units, "parts": len(stats)}
    return piece_call(first_piece_kernel, outs, (*stats, *operands), tall, cols, count, extra)


def next_piece(factors, operands, tall, cols):
    count = operands[0].shape[1]
    return piece_call(last_part, (), (*factors, *operands), tall, cols, count, {})[0]


def losses_kernel(first_ref, second_ref, out_ref, buffer, sem):
    buffer[:, 0:1] = first_ref[:, 0:1]
    buffer[:, 1:2] = second_ref[:, 0:1]
    copy = pltpu.make_async_copy(buffer, out_ref, sem)
    copy.start()
    copy.wait()


def losses_out(first, second):
    whole = pl.BlockSpec(memory_space=pltpu.VMEM)
    return pl.pallas_call(
        losses_kernel,
        out_shape=pltpu.HBM((1, 2), F32),
        in_specs=[whole, whole],
        out_specs=pl.BlockSpec(memory_space=pl.ANY),
        scratch_shapes=[pltpu.VMEM((1, 2), F32), pltpu.SemaphoreType.DMA(())],
        compiler_params=pltpu.CompilerParams(vmem_limit_bytes=KERNEL_VMEM),
        name="losses",
    )(first, second)


def mean_kernel(own_ref, peer_ref, *refs, tall, cols, parts):
    out_ref, buffer, sems = refs[-3:]
    height, block = own_ref.shape
    rows = height // parts
    step = min(256 if block <= LANES else 64, rows)

    def copy(at):
        part = pl.ds(pl.multiple_of(at * rows, rows), rows)
        there = pl.ds(pl.multiple_of(tall.start + at * rows, rows), rows)
        return pltpu.make_async_copy(buffer.at[part, :], out_ref.at[there, cols], sems.at[at])

    def one(at, carry):
        def inner(sub, carry):
            part = pl.ds(pl.multiple_of(at * rows + sub * step, step), step)
            buffer[part, :] = (
                (own_ref[part, :].astype(F32) + peer_ref[part, :].astype(F32)) * 0.5
            ).astype(BF16)
            return carry

        lax.fori_loop(0, rows // step, inner, 0)
        copy(at).start()
        return carry

    lax.fori_loop(0, parts, one, 0)
    for at in range(parts):
        copy(at).wait()


def mean_into(out, own, peer, shape, tall, cols):
    height, block = own.shape
    parts = 4 if height % (4 * LANES) == 0 else 1
    whole = pl.BlockSpec(memory_space=pltpu.VMEM)
    anywhere = pl.BlockSpec(memory_space=pl.ANY)
    return pl.pallas_call(
        functools.partial(mean_kernel, tall=tall, cols=cols, parts=parts),
        out_shape=jax.ShapeDtypeStruct(shape, BF16),
        in_specs=[whole, whole] + ([] if out is None else [anywhere]),
        out_specs=anywhere,
        scratch_shapes=[
            pltpu.VMEM((height, block), BF16),
            pltpu.SemaphoreType.DMA((parts,)),
        ],
        input_output_aliases={} if out is None else {2: 0},
        compiler_params=pltpu.CompilerParams(vmem_limit_bytes=KERNEL_VMEM),
        cost_estimate=pl.CostEstimate(
            flops=2 * height * block, bytes_accessed=6 * height * block, transcendentals=0
        ),
        name="mean",
    )(*([own, peer] + ([] if out is None else [out])))


def tree_sum(parts):
    while len(parts) > 1:
        parts = [parts[at] + parts[at + 1] for at in range(0, len(parts), 2)]
    return parts[0]


def everyones(array, axis):
    devices = lax.axis_size(axis)
    if devices & (devices - 1):
        return [lax.psum(array, axis)]
    return [array] + [
        lax.ppermute(array, axis, [(i, i ^ flip) for i in range(devices)])
        for flip in range(1, devices)
    ]


def shifted(array, axis, by):
    devices = lax.axis_size(axis)
    return lax.ppermute(array, axis, [(i, (i + by) % devices) for i in range(devices)])


def shards(weight, tokens, cotangent, batch_order, step_index):
    weight, tokens, target, order = weight[0], tokens[0], cotangent[0], batch_order[0]
    width, columns = weight.shape
    units = columns * lax.axis_size("tp")
    levels = lax.axis_size("rep").bit_length() - 1
    hop_level = lax.rem(step_index[0], levels)

    pieces = chunks_of(width, columns)

    def chain(exponent):
        def run(order, tokens, weight, target):
            hidden, flipped, stats, tokens, weight, target = forward(order, tokens, weight, target)
            stats = everyones(stats, "tp")
            gradient, hidden, flipped, stats, loss_first = middle(
                stats, flipped, tokens, weight, hidden, target, units
            )
            stats = everyones(stats, "tp")
            finals, peers = [], []
            operands = (flipped, weight, gradient, hidden, target)
            for at, piece in enumerate(pieces):
                if at == 0:
                    final, *factors, loss_second = first_piece(stats, operands, units, *piece)
                else:
                    final = next_piece(factors, operands, *piece)
                finals.append(final)
                peers.append(shifted(final, "rep", 2**exponent))
            out = None
            for piece, final, peer in zip(pieces, finals, peers):
                out = mean_into(out, final, peer, weight.shape, *piece)
            return out, losses_out(loss_first, loss_second)

        return run

    averaged, losses = lax.switch(
        hop_level, [chain(exponent) for exponent in range(levels)], order, tokens, weight, target
    )
    return (averaged[None], losses)


def solution(mesh):
    placed = (
        P("rep", None, "tp"),
        P("rep", None, None, None),
        P("rep", None, None, "tp"),
        P("rep", None),
        P(),
    )
    return jax.shard_map(
        shards,
        mesh=mesh,
        in_specs=placed,
        out_specs=(P("rep", None, "tp"), P("rep", None)),
        check_vma=False,
    )
```
